128 devices in a mesh: dom: 16 (over x, y), cls: 8 (over z, core).
Axes of the slice: x: 4, y: 4, z: 4, core: 2. Of those that a mesh axis runs over, the one named last changes fastest.
Arguments:
- stack: bfloat16 [32768, 2, 64, 128], P(('dom', 'cls')), may hold values from -6 to 6
- batch_index: int32 [16384], P(('dom', 'cls')), may hold values from 0 to 255, as said below
- best_class: int32 [16384], P(('dom', 'cls')), may hold values from 0 to 511, as said below
- best_rot: int32 [16384], P(('dom', 'cls')), may hold values from 0 to 63
- best_shift: int32 [16384, 2], P(('dom', 'cls')), may hold values from -4 to 4
- ctf: bfloat16 [16384, 64], P(('dom', 'cls')), may hold values from -1 to 1
- averages: float32 [512, 2, 64, 128], P(('dom', 'cls')), may hold values from -6 to 6
- velocity: float32 [512, 2, 64, 128], P(('dom', 'cls')), may hold values from -3 to 3
Outputs:
- new_averages: float32 [512, 2, 64, 128], P(('dom', 'cls'))
- new_velocity: float32 [512, 2, 64, 128], P(('dom', 'cls'))
- errors: float32 [16384], P(('dom', 'cls'))
The draws below stay inside these ranges and needn't reach their ends.
Inputs may be any that keep to these rules, and one draw needn't show every extreme that they name: `batch_index`: each aligned block of 128 entries (one device's particles) holds distinct row numbers into that device's own 256 rows of stack. `best_class`: classes c with equal c // 32 form a group. In each aligned block of 128 entries (one device's particles) at most 16 entries name classes of one group, and some group is named by exactly 16 entries of that block.
All inputs are finite; a program needn't handle non-finite values.
Results may differ from the reference program's by a relative error of at most 0.0026.
Values may be sent and summed in bfloat16 or wider, within the bound.
No kernel may reach another device: no remote copies, remote signals or barrier semaphores. Data moves between devices by JAX's collectives and lax.ppermute only.
A program may use at most 128 MiB of HBM per device.

```python
import jax
import jax.numpy as jnp
from jax import lax

IMG = 128
CYCLES = 64
ROTS = 64
ANGLES = 128
SHIFT = 4
CLASSES = 512
P_DEV = 128
PARTS_SIZE = 16384
STACK_DEV = 256
CAP = 16
N_DOM = 16
N_CLS = 8
DEVICES = 128


def draw_batch_index(key, part):
    blocks = PARTS_SIZE // P_DEV

    def single(block):
        order = jax.random.permutation(jax.random.fold_in(key, block), STACK_DEV)
        return order[:P_DEV].astype(jnp.int32)
    return jax.vmap(single)(jnp.arange(blocks)).reshape(PARTS_SIZE)


def draw_best_class(key, part):
    blocks = PARTS_SIZE // P_DEV
    column = CLASSES // N_DOM
    per_device = CLASSES // (N_DOM * N_CLS)

    def single(block):
        group = block % N_CLS
        hottest = jax.random.randint(jax.random.fold_in(key, 7919 + group), (), 0, N_DOM)
        inner = jax.random.fold_in(key, block)
        order = jax.random.permutation(jax.random.fold_in(inner, 1), P_DEV)
        owner = jnp.where(order < CAP, hottest, (hottest + 1 + (order - CAP) % (N_DOM - 1)) % N_DOM)
        within = jax.random.randint(jax.random.fold_in(inner, 2), (P_DEV,), 0, N_CLS)
        chosen = jax.random.randint(jax.random.fold_in(inner, 3), (P_DEV,), 0, per_device)
        return (owner * column + within * per_device + chosen).astype(jnp.int32)
    return jax.vmap(single)(jnp.arange(blocks)).reshape(PARTS_SIZE)


def place_ends(values, rng, smallest, top_value):
    longest = values.shape.index(max(values.shape))
    spots = []
    for shift in (0, 1):
        where = [jax.random.randint(jax.random.fold_in(rng, axis), (), 0, length) for axis, length in enumerate(values.shape)]
        where[longest] = (where[longest] + shift) % values.shape[longest]
        spots.append(tuple(where))
    return values.at[spots[0]].set(smallest).at[spots[1]].set(top_value)


def shard_levels(rng, shape, split, smallest, top_value):
    def one(dim, parts):
        steps = jax.random.uniform(jax.random.fold_in(jax.random.fold_in(rng, 6), dim), (parts,), jnp.float32, smallest / len(split), top_value / len(split))
        return jnp.repeat(jnp.exp(steps), shape[dim] // parts).reshape((-1,) + (1,) * (len(shape) - dim - 1))

    factor_of = one(*split[0])
    for cut in split[1:]:
        factor_of = factor_of * one(*cut)
    return factor_of


def bell_draw(key, shape, spread, bound, shards=(), dtype=jnp.bfloat16):
    entries = jax.random.normal(key, shape, jnp.float32) * spread
    if len(shards) > 0:
        entries = shard_levels(key, shape, shards, -0.22, 0.18) * entries
    return jnp.clip(entries, min=-bound, max=bound).astype(dtype)


def setup_inputs(seed: int = 0) -> dict:
    arg_keys = jax.random.split(jax.random.key(seed), 9)
    stack = bell_draw(arg_keys[0], (STACK_DEV * DEVICES, 2, CYCLES, ANGLES), 1.0, 6.0, ((0, 128),))
    batch_index = draw_batch_index(jax.random.fold_in(arg_keys[8], 71), 0)
    best_class = draw_best_class(jax.random.fold_in(arg_keys[8], 71), 0)
    best_rot = place_ends(jax.random.randint(arg_keys[3], (PARTS_SIZE,), 0, ROTS), jax.random.fold_in(arg_keys[3], 1), 0, ROTS - 1).astype(jnp.int32)
    best_shift = place_ends(jax.random.randint(arg_keys[4], (PARTS_SIZE, 2), 0 - SHIFT, SHIFT + 1), jax.random.fold_in(arg_keys[4], 1), 0 - SHIFT, SHIFT).astype(jnp.int32)
    ctf = jnp.clip(jax.random.uniform(arg_keys[5], (PARTS_SIZE, CYCLES), jnp.float32, -1.0, 1.0) * shard_levels(arg_keys[5], (PARTS_SIZE, CYCLES), ((0, 128),), -0.4, 0.0), -1.0, 1.0).astype(jnp.bfloat16)
    averages = bell_draw(arg_keys[6], (CLASSES, 2, CYCLES, ANGLES), 1.0, 6.0, ((0, 128),), jnp.float32)
    velocity = bell_draw(arg_keys[7], (CLASSES, 2, CYCLES, ANGLES), 0.5, 3.0, ((0, 128),), jnp.float32)
    return {"stack": stack, "batch_index": batch_index, "best_class": best_class, "best_rot": best_rot, "best_shift": best_shift, "ctf": ctf, "averages": averages, "velocity": velocity}


TWO_PI = 6.283185307179586
MOMENTUM = 0.9
RATE = 0.5
RIDGE = 1.0


def align_rows(rows, rotation, shift):
    cycles = rows.shape[2]
    angles = rows.shape[3]
    radius = jnp.arange(cycles).astype(jnp.float32) + 1.0
    theta = TWO_PI * jnp.arange(angles).astype(jnp.float32) / angles
    shift_x = shift[:, 0].astype(jnp.float32)
    shift_y = shift[:, 1].astype(jnp.float32)
    along = jnp.cos(theta)[None, None, :] * shift_x[:, None, None] + jnp.sin(theta)[None, None, :] * shift_y[:, None, None]
    phase = TWO_PI * radius[None, :, None] * along / IMG
    cosine = jnp.cos(phase)
    sine = jnp.sin(phase)
    real = rows[:, 0].astype(jnp.float32)
    imag = rows[:, 1].astype(jnp.float32)
    turned = jnp.stack([cosine * real - sine * imag, sine * real + cosine * imag], axis=1)
    index = (jnp.arange(angles).astype(jnp.int32)[None, :] + 2 * rotation.astype(jnp.int32)[:, None]) % angles
    index = jnp.broadcast_to(index[:, None, None, :], turned.shape).astype(jnp.int32)
    return jnp.take_along_axis(turned, index, axis=3).astype(jnp.bfloat16)


def reference(stack, batch_index, best_class, best_rot, best_shift, ctf, averages, velocity):
    blocks = PARTS_SIZE // P_DEV
    models = averages.astype(jnp.bfloat16)
    stored = stack.reshape(blocks, STACK_DEV, 2, CYCLES, ANGLES)

    def one_block(carry, pieces):
        grads, weights = carry
        store, index, classes, rotation, shift, gamma = pieces
        rows = jnp.take(store, index, axis=0)
        aligned = align_rows(rows, rotation, shift)
        model = jnp.take(models, classes, axis=0).astype(jnp.float32)
        gamma_wide = gamma.astype(jnp.float32)[:, None, :, None]
        resid = aligned.astype(jnp.float32) - gamma_wide * model
        error = jnp.mean(resid * resid, axis=(1, 2, 3))
        term = (gamma_wide * resid).astype(jnp.bfloat16)
        grads = grads + jax.ops.segment_sum(term.astype(jnp.float32), classes, num_segments=CLASSES)
        squares = gamma.astype(jnp.float32) * gamma.astype(jnp.float32)
        weights = weights + jax.ops.segment_sum(squares, classes, num_segments=CLASSES)
        return (grads, weights), error

    start = (jnp.zeros((CLASSES, 2, CYCLES, ANGLES), jnp.float32), jnp.zeros((CLASSES, CYCLES), jnp.float32))
    pieces = (stored, batch_index.reshape(blocks, P_DEV), best_class.reshape(blocks, P_DEV),
              best_rot.reshape(blocks, P_DEV), best_shift.reshape(blocks, P_DEV, 2), ctf.reshape(blocks, P_DEV, CYCLES))
    (grads, weights), errors = lax.scan(one_block, start, pieces)
    step = (grads - RIDGE * averages) / (weights[:, None, :, None] + RIDGE)
    new_velocity = MOMENTUM * velocity + step
    new_averages = averages + RATE * new_velocity
    return new_averages, new_velocity, errors.reshape(PARTS_SIZE)
```

```python
import numpy as np
import jax
import jax.numpy as jnp
from jax import lax
from jax.experimental import pallas as pl
from jax.experimental.pallas import tpu as pltpu
from jax.sharding import PartitionSpec as P

IMG = 128
TOP_SHIFT = 4
MOMENTUM = 0.9
RATE = 0.5
RIDGE = 1.0
BATCH = 16
SOURCES = 16
AUX = 8
HALF_CLASSES = 256


def phase_tables(cycles, angles):
    radius = np.arange(1, cycles + 1, dtype=np.float64)[:, None]
    theta = 2.0 * np.pi * np.arange(angles, dtype=np.float64)[None, :] / angles
    shifts = np.arange(-TOP_SHIFT, TOP_SHIFT + 1, dtype=np.float64)[:, None, None]
    tables = []
    for along in (np.cos(theta), np.sin(theta)):
        phase = 2.0 * np.pi * radius * along / IMG * shifts
        tables.append(np.stack([np.cos(phase), np.sin(phase)], axis=1))
    return np.stack(tables).astype(np.float32)


def align_kernel(index_ref, rot_ref, shift_ref, *refs):
    blocks = refs[:BATCH]
    table_ref, ctf_ref, class_ref, averages_ref, out_ref, turned_ref = refs[BATCH:]
    step = pl.program_id(0)
    cycles, angles = table_ref.shape[3], table_ref.shape[4]
    grid_rows = 2 * cycles
    count = ctf_ref.shape[0]
    for j in range(BATCH):
        particle = step * BATCH + j
        sx = shift_ref[0, particle] + TOP_SHIFT
        sy = shift_ref[1, particle] + TOP_SHIFT
        back = (angles - 2 * rot_ref[particle]) % angles
        xr, xi = table_ref[0, sx, 0], table_ref[0, sx, 1]
        yr, yi = table_ref[1, sy, 0], table_ref[1, sy, 1]
        cosine = xr * yr - xi * yi
        sine = xr * yi + xi * yr
        real = blocks[j][0, 0].astype(jnp.float32)
        imag = blocks[j][0, 1].astype(jnp.float32)
        base = j * grid_rows
        turned_ref[base : base + cycles, :] = pltpu.roll(cosine * real - sine * imag, back, 1)
        turned_ref[base + cycles : base + grid_rows, :] = pltpu.roll(
            sine * real + cosine * imag, back, 1
        )
    first = pl.multiple_of(step * BATCH, BATCH)

    def spread(r, carry):
        got = turned_ref[pl.ds(r, BATCH, stride=grid_rows), :]
        out_ref[r, pl.ds(first, BATCH), :] = got.astype(jnp.bfloat16)
        return carry

    lax.fori_loop(0, grid_rows, spread, 0, unroll=16)

    @pl.when(step == pl.num_programs(0) - 1)
    def _():
        classes = (class_ref[...] - HALF_CLASSES).astype(jnp.float32)
        turned_ref[0:grid_rows, :] = jnp.broadcast_to(classes, (grid_rows, angles))
        gamma = ctf_ref[...].astype(jnp.float32).T
        turned_ref[grid_rows : grid_rows + cycles, :] = gamma
        turned_ref[grid_rows + cycles : 2 * grid_rows, :] = gamma
        owned = averages_ref.shape[0]
        for j in range(owned):
            turned_ref[(2 + j) * grid_rows : (3 + j) * grid_rows, :] = averages_ref[j]
        for j in range(2 + owned, AUX):
            turned_ref[j * grid_rows : (j + 1) * grid_rows, :] = jnp.zeros(
                (grid_rows, angles), jnp.float32
            )

        def spread_aux(r, carry):
            got = turned_ref[pl.ds(r, AUX, stride=grid_rows), :]
            out_ref[r, pl.ds(count, AUX), :] = got.astype(jnp.bfloat16)
            return carry

        lax.fori_loop(0, grid_rows, spread_aux, 0, unroll=16)


def align(stack, batch_index, best_class, best_rot, best_shift, ctf, averages):
    count = batch_index.shape[0]
    cycles, angles = stack.shape[2], stack.shape[3]
    grid_rows = 2 * cycles
    owned = averages.shape[0]

    def pick(j):
        return pl.BlockSpec(
            (1, 2, cycles, angles), lambda i, index, rot, shift: (index[i * BATCH + j], 0, 0, 0)
        )

    def whole(shape):
        return pl.BlockSpec(shape, lambda i, index, rot, shift: (0,) * len(shape))

    table = jnp.asarray(phase_tables(cycles, angles))
    return pl.pallas_call(
        align_kernel,
        out_shape=jax.ShapeDtypeStruct((grid_rows, count + AUX, angles), jnp.bfloat16),
        grid_spec=pltpu.PrefetchScalarGridSpec(
            num_scalar_prefetch=3,
            grid=(count // BATCH,),
            in_specs=[pick(j) for j in range(BATCH)]
            + [
                whole(table.shape),
                whole((count, cycles)),
                whole((1, count)),
                whole((owned, grid_rows, angles)),
            ],
            out_specs=whole((grid_rows, count + AUX, angles)),
            scratch_shapes=[pltpu.VMEM((BATCH * grid_rows, angles), jnp.float32)],
        ),
        compiler_params=pltpu.CompilerParams(
            dimension_semantics=("arbitrary",), vmem_limit_bytes=48 << 20
        ),
        name="align",
    )(
        batch_index,
        best_rot,
        best_shift.T,
        *([stack] * BATCH),
        table,
        ctf,
        best_class.reshape(1, count),
        averages.reshape(owned, grid_rows, angles),
    )


def classes_kernel(
    rows_ref,
    aux_ref,
    out_ref,
    aux32_ref,
    class_ref,
    gamma_ref,
    model_ref,
    sums_ref,
    grads_ref,
    weights_ref,
    error_ref,
):
    step = pl.program_id(0)
    devices, angles = aux_ref.shape[0], aux_ref.shape[2]
    count = rows_ref.shape[1]
    classes = model_ref.shape[0]
    owned = classes // devices

    @pl.when(step == 0)
    def _():
        aux32_ref[...] = aux_ref[...].astype(jnp.float32).reshape(devices * AUX, angles)
        class_ref[...] = aux32_ref[pl.ds(0, devices, stride=AUX), :]
        gamma_ref[...] = aux32_ref[pl.ds(1, devices, stride=AUX), :]
        for j in range(owned):
            grads_ref[pl.ds(j, devices, stride=owned), :] = aux32_ref[
                pl.ds(2 + j, devices, stride=AUX), :
            ]
        model_ref[...] = grads_ref[...].astype(jnp.bfloat16)
        sums_ref[...] = jnp.zeros(sums_ref.shape, jnp.float32)

    first = pl.multiple_of(step * SOURCES, SOURCES)
    class_block = class_ref[pl.ds(first, SOURCES), :]
    gamma_block = gamma_ref[pl.ds(first, SOURCES), :]
    class_turned = class_block.T
    gamma_turned = gamma_block.T
    down = lax.broadcasted_iota(jnp.int32, (classes, count), 0) - HALF_CLASSES
    down = down.astype(jnp.float32).astype(jnp.bfloat16)
    across = lax.broadcasted_iota(jnp.int32, (count, classes), 1) - HALF_CLASSES
    across = across.astype(jnp.float32).astype(jnp.bfloat16)
    zero = jnp.zeros((), jnp.bfloat16)
    one = jnp.ones((), jnp.bfloat16)
    error_columns = []
    for pair in range(SOURCES // 2):
        tables = []
        values = []
        for b in (2 * pair, 2 * pair + 1):
            rows = rows_ref[b]
            names = class_block[b : b + 1, :].astype(jnp.bfloat16)
            gammas = gamma_block[b : b + 1, :].astype(jnp.bfloat16)
            tables.append(jnp.where(down == names, gammas, zero))
            gamma_wide = jnp.broadcast_to(gamma_turned[:, b : b + 1], (count, angles))
            values.append(jnp.concatenate([rows, gamma_wide.astype(jnp.bfloat16)], axis=1))
            names_wide = jnp.broadcast_to(class_turned[:, b : b + 1], (count, classes))
            choice = jnp.where(names_wide.astype(jnp.bfloat16) == across, one, zero)
            model = jnp.dot(choice, model_ref[...], preferred_element_type=jnp.float32)
            resid = rows.astype(jnp.float32) - gamma_wide * model
            error_columns.append(jnp.sum(resid * resid, axis=1, keepdims=True))
        sums_ref[...] += jnp.dot(
            jnp.concatenate(tables, axis=1),
            jnp.concatenate(values, axis=0),
            preferred_element_type=jnp.float32,
        )
    error_ref[pl.ds(first, SOURCES), :] = jnp.concatenate(error_columns, axis=1).T

    @pl.when(step == pl.num_programs(0) - 1)
    def _():
        sums = sums_ref[:, 0:angles]
        weights = sums_ref[:, angles : 2 * angles]
        weights_ref[...] = weights
        grads_ref[...] = sums - weights * model_ref[...].astype(jnp.float32)
        share = angles // owned
        lane = lax.broadcasted_iota(jnp.int32, (devices, angles), 1) // share
        packed = jnp.zeros((devices, angles), jnp.float32)
        for j in range(owned):
            out_ref[pl.ds(j, devices, stride=AUX), :] = grads_ref[
                pl.ds(j, devices, stride=owned), :
            ]
            mine = weights_ref[pl.ds(j, devices, stride=owned), :]
            packed = jnp.where(lane == j, mine, packed)
        out_ref[pl.ds(owned, devices, stride=AUX), :] = packed
        out_ref[pl.ds(owned + 1, devices, stride=AUX), :] = error_ref[...]
        for j in range(owned + 2, AUX):
            out_ref[pl.ds(j, devices, stride=AUX), :] = jnp.zeros((devices, angles), jnp.float32)


def class_sums(received, owned):
    devices, rows, angles = received.shape
    count = rows - AUX
    classes = owned * devices
    return pl.pallas_call(
        classes_kernel,
        out_shape=jax.ShapeDtypeStruct((devices * AUX, angles), jnp.float32),
        grid=(devices // SOURCES,),
        in_specs=[
            pl.BlockSpec((SOURCES, count, angles), lambda i: (i, 0, 0)),
            pl.BlockSpec((devices, AUX, angles), lambda i: (0, count // AUX, 0)),
        ],
        out_specs=pl.BlockSpec((devices * AUX, angles), lambda i: (0, 0)),
        scratch_shapes=[
            pltpu.VMEM((devices * AUX, angles), jnp.float32),
            pltpu.VMEM((devices, count), jnp.float32),
            pltpu.VMEM((devices, count), jnp.float32),
            pltpu.VMEM((classes, angles), jnp.bfloat16),
            pltpu.VMEM((classes, 2 * angles), jnp.float32),
            pltpu.VMEM((classes, angles), jnp.float32),
            pltpu.VMEM((classes, angles), jnp.float32),
            pltpu.VMEM((devices, count), jnp.float32),
        ],
        compiler_params=pltpu.CompilerParams(
            dimension_semantics=("arbitrary",), vmem_limit_bytes=48 << 20
        ),
        name="class_sums",
    )(received, received)


def update_kernel(back_ref, averages_ref, velocity_ref, new_averages_ref, new_velocity_ref, error_ref):
    owned, grid_rows, angles = averages_ref.shape
    share = angles // owned
    packed = back_ref[pl.ds(owned, grid_rows, stride=AUX), :]
    for j in range(owned):
        grads = back_ref[pl.ds(j, grid_rows, stride=AUX), :]
        weights = jnp.broadcast_to(packed[:, j * share : j * share + 1], (grid_rows, angles))
        old = averages_ref[j]
        step = (grads - RIDGE * old) / (weights + RIDGE)
        moved = MOMENTUM * velocity_ref[j] + step
        new_velocity_ref[j] = moved
        new_averages_ref[j] = old + RATE * moved
    parts = back_ref[pl.ds(owned + 1, grid_rows, stride=AUX), :]
    error_ref[...] = jnp.sum(parts, axis=0, keepdims=True) / (grid_rows * angles)


def update(back, averages, velocity, count):
    owned = averages.shape[0]
    grid_rows, angles = 2 * averages.shape[2], averages.shape[3]
    flat = (owned, grid_rows, angles)
    new_averages, new_velocity, errors = pl.pallas_call(
        update_kernel,
        out_shape=(
            jax.ShapeDtypeStruct(flat, jnp.float32),
            jax.ShapeDtypeStruct(flat, jnp.float32),
            jax.ShapeDtypeStruct((1, count), jnp.float32),
        ),
        compiler_params=pltpu.CompilerParams(vmem_limit_bytes=48 << 20),
        name="update",
    )(back, averages.reshape(flat), velocity.reshape(flat))
    return (
        new_averages.reshape(averages.shape),
        new_velocity.reshape(averages.shape),
        errors.reshape(count),
    )


def on_device(stack, batch_index, best_class, best_rot, best_shift, ctf, averages, velocity):
    everyone = ("dom", "cls")
    sent = align(stack, batch_index, best_class, best_rot, best_shift, ctf, averages)
    received = lax.all_to_all(sent, everyone, split_axis=0, concat_axis=0, tiled=True)
    partial = class_sums(received, averages.shape[0])
    devices = received.shape[0]
    partial = partial.reshape(devices, AUX, received.shape[2])
    back = lax.all_to_all(partial, everyone, split_axis=0, concat_axis=0, tiled=True)
    back = back.reshape(devices * AUX, received.shape[2])
    return update(back, averages, velocity, batch_index.shape[0])


def solution(mesh):
    whole = ("dom", "cls")
    in_specs = (
        P(whole, None, None, None),
        P(whole),
        P(whole),
        P(whole),
        P(whole, None),
        P(whole, None),
        P(whole, None, None, None),
        P(whole, None, None, None),
    )
    out_specs = (P(whole, None, None, None), P(whole, None, None, None), P(whole))
    return jax.shard_map(
        on_device, mesh=mesh, in_specs=in_specs, out_specs=out_specs, check_vma=False
    )
```

```python
import numpy as np
import jax
import jax.numpy as jnp
from jax import lax
from jax.experimental import pallas as pl
from jax.experimental.pallas import tpu as pltpu
from jax.sharding import PartitionSpec as P

IMG = 128
TOP_SHIFT = 4
MOMENTUM = 0.9
RATE = 0.5
RIDGE = 1.0
BATCH = 16
SOURCES = 16
AUX = 8
PAD = 8
TILE = 16
HALF_CLASSES = 256


def phase_tables(cycles, angles):
    radius = np.arange(1, cycles + 1, dtype=np.float64)[:, None]
    theta = 2.0 * np.pi * np.arange(angles, dtype=np.float64)[None, :] / angles
    shifts = np.arange(-TOP_SHIFT, TOP_SHIFT + 1, dtype=np.float64)[:, None, None]
    tables = []
    for along in (np.cos(theta), np.sin(theta)):
        phase = 2.0 * np.pi * radius * along / IMG * shifts
        tables.append(np.stack([np.cos(phase), np.sin(phase)], axis=1))
    return np.stack(tables).astype(np.float32)


def align_kernel(
    index_hbm,
    rot_hbm,
    shift_hbm,
    stack_hbm,
    table_hbm,
    ctf_hbm,
    class_hbm,
    averages_hbm,
    out_ref,
    rows_ref,
    turned_ref,
    table_ref,
    index_ref,
    rot_ref,
    shift_ref,
    ctf_ref,
    class_ref,
    averages_ref,
    row_sems,
    sems,
):
    cycles, angles = table_ref.shape[3], table_ref.shape[4]
    grid_rows = 2 * cycles
    count = rows_ref.shape[0]
    chunks = count // BATCH
    owned = averages_ref.shape[0]
    pitch = grid_rows + PAD
    pairs = (
        (index_hbm, index_ref),
        (table_hbm, table_ref),
        (rot_hbm, rot_ref),
        (shift_hbm, shift_ref),
        (ctf_hbm, ctf_ref),
        (class_hbm, class_ref),
        (averages_hbm, averages_ref),
    )
    copies = [pltpu.make_async_copy(a, b, sems.at[n]) for n, (a, b) in enumerate(pairs)]
    for copy in copies:
        copy.start()
    copies[0].wait()

    def issue(i, carry):
        for j in range(BATCH):
            pltpu.make_async_copy(
                stack_hbm.at[index_ref[i * BATCH + j]], rows_ref.at[i * BATCH + j], row_sems.at[i]
            ).start()
        return carry

    lax.fori_loop(0, chunks, issue, 0)
    for copy in copies[2:]:
        copy.wait()

    classes = (class_ref[...] - HALF_CLASSES).astype(jnp.float32)
    gamma = ctf_ref[...].astype(jnp.float32)
    turned_ref[0:grid_rows, :] = jnp.broadcast_to(classes, (grid_rows, angles))
    turned_ref[pitch : pitch + cycles, :] = gamma
    turned_ref[pitch + cycles : pitch + grid_rows, :] = gamma
    for j in range(owned):
        turned_ref[(2 + j) * pitch : (2 + j) * pitch + grid_rows, :] = averages_ref[j]
    for j in range(2 + owned, AUX):
        turned_ref[j * pitch : j * pitch + grid_rows, :] = jnp.zeros(
            (grid_rows, angles), jnp.float32
        )

    def spread_aux(r, carry):
        got = turned_ref[pl.ds(r, AUX, stride=pitch), :]
        out_ref[r, pl.ds(count, AUX), :] = got.astype(jnp.bfloat16)
        return carry

    lax.fori_loop(0, grid_rows, spread_aux, 0, unroll=32)
    copies[1].wait()

    def chunk(i, carry):
        first = pl.multiple_of(i * BATCH, BATCH)
        pltpu.make_async_copy(
            stack_hbm.at[pl.ds(0, BATCH)], rows_ref.at[pl.ds(first, BATCH)], row_sems.at[i]
        ).wait()
        for j in range(BATCH):
            particle = i * BATCH + j
            sx = shift_ref[0, particle] + TOP_SHIFT
            sy = shift_ref[1, particle] + TOP_SHIFT
            back = (angles - 2 * rot_ref[particle]) % angles
            xr, xi = table_ref[0, sx, 0], table_ref[0, sx, 1]
            yr, yi = table_ref[1, sy, 0], table_ref[1, sy, 1]
            cosine = xr * yr - xi * yi
            sine = xr * yi + xi * yr
            real = rows_ref[particle, 0].astype(jnp.float32)
            imag = rows_ref[particle, 1].astype(jnp.float32)
            base = j * pitch
            turned_ref[base : base + cycles, :] = pltpu.roll(
                cosine * real - sine * imag, back, 1
            )
            turned_ref[base + cycles : base + grid_rows, :] = pltpu.roll(
                sine * real + cosine * imag, back, 1
            )

        def spread(r, inner):
            got = turned_ref[pl.ds(r, BATCH, stride=pitch), :]
            out_ref[r, pl.ds(first, BATCH), :] = got.astype(jnp.bfloat16)
            return inner

        lax.fori_loop(0, grid_rows, spread, 0, unroll=32)
        return carry

    lax.fori_loop(0, chunks, chunk, 0)


def align(stack, batch_index, best_class, best_rot, best_shift, ctf, averages):
    count = batch_index.shape[0]
    cycles, angles = stack.shape[2], stack.shape[3]
    grid_rows = 2 * cycles
    owned = averages.shape[0]
    table = jnp.asarray(phase_tables(cycles, angles))
    operands = (
        batch_index,
        best_rot,
        best_shift.T,
        stack,
        table,
        ctf.T,
        best_class.reshape(1, count),
        averages.reshape(owned, grid_rows, angles),
    )
    return pl.pallas_call(
        align_kernel,
        out_shape=jax.ShapeDtypeStruct((grid_rows, count + AUX, angles), jnp.bfloat16),
        in_specs=[pl.BlockSpec(memory_space=pltpu.HBM)] * len(operands),
        out_specs=pl.BlockSpec(memory_space=pltpu.VMEM),
        scratch_shapes=[
            pltpu.VMEM((count, 2, cycles, angles), jnp.bfloat16),
            pltpu.VMEM((BATCH * (grid_rows + PAD), angles), jnp.float32),
            pltpu.VMEM(table.shape, jnp.float32),
            pltpu.SMEM((count,), jnp.int32),
            pltpu.SMEM((count,), jnp.int32),
            pltpu.SMEM((2, count), jnp.int32),
            pltpu.VMEM((cycles, count), jnp.bfloat16),
            pltpu.VMEM((1, count), jnp.int32),
            pltpu.VMEM((owned, grid_rows, angles), jnp.float32),
            pltpu.SemaphoreType.DMA((count // BATCH,)),
            pltpu.SemaphoreType.DMA((7,)),
        ],
        compiler_params=pltpu.CompilerParams(vmem_limit_bytes=48 << 20),
        name="align",
    )(*[pltpu.with_memory_space_constraint(x, pltpu.HBM) for x in operands])


def classes_kernel(
    rows_ref,
    aux_ref,
    out_ref,
    aux32_ref,
    class_ref,
    gamma_ref,
    model_ref,
    turned_model_ref,
    sums_ref,
    grads_ref,
    weights_ref,
    error_ref,
):
    step = pl.program_id(0)
    devices, angles = aux_ref.shape[0], aux_ref.shape[2]
    count = rows_ref.shape[1]
    classes = model_ref.shape[0]
    owned = classes // devices

    @pl.when(step == 0)
    def _():
        aux32_ref[...] = aux_ref[...].astype(jnp.float32).reshape(devices * AUX, angles)
        class_ref[...] = aux32_ref[pl.ds(0, devices, stride=AUX), :]
        gamma_ref[...] = aux32_ref[pl.ds(1, devices, stride=AUX), :]
        for j in range(owned):
            model_ref[pl.ds(j, devices, stride=owned), :] = aux32_ref[
                pl.ds(2 + j, devices, stride=AUX), :
            ]
        turned_model_ref[...] = model_ref[...].T.astype(jnp.bfloat16)
        sums_ref[...] = jnp.zeros(sums_ref.shape, jnp.float32)

    first = pl.multiple_of(step * SOURCES, SOURCES)
    class_block = class_ref[pl.ds(first, SOURCES), :]
    gamma_block = gamma_ref[pl.ds(first, SOURCES), :]
    down = lax.broadcasted_iota(jnp.int32, (classes, count), 0) - HALF_CLASSES
    down = down.astype(jnp.float32).astype(jnp.bfloat16)
    zero = jnp.zeros((), jnp.bfloat16)
    last_dims = (((1,), (1,)), ((), ()))
    errors = []
    for pair in range(SOURCES // 2):
        tables = []
        gammas = []
        for b in (2 * pair, 2 * pair + 1):
            name = class_block[b : b + 1, :].astype(jnp.bfloat16)
            gamma = gamma_block[b : b + 1, :]
            tables.append(jnp.where(down == name, gamma.astype(jnp.bfloat16), zero))
            gammas.append(jnp.broadcast_to(gamma, (TILE, count)))
        table = jnp.concatenate(tables, axis=1)
        rows = rows_ref[2 * pair : 2 * pair + 2].reshape(2 * count, angles)
        turned = rows.astype(jnp.float32).T
        resid = turned - jnp.dot(
            turned_model_ref[...], table, preferred_element_type=jnp.float32
        )
        error = jnp.sum(resid * resid, axis=0, keepdims=True)
        errors += [error[:, 0:count], error[:, count : 2 * count]]
        values = jnp.concatenate([turned, jnp.concatenate(gammas, axis=1)], axis=0)
        sums_ref[...] += lax.dot_general(
            values.astype(jnp.bfloat16), table, last_dims, preferred_element_type=jnp.float32
        )
    error_ref[pl.ds(first, SOURCES), :] = jnp.concatenate(errors, axis=0)

    @pl.when(step == pl.num_programs(0) - 1)
    def _():
        weights = jnp.broadcast_to(sums_ref[angles : angles + 1, :], (angles, classes)).T
        weights_ref[...] = weights
        grads_ref[...] = sums_ref[0:angles, :].T - weights * model_ref[...]
        share = angles // owned
        lane = lax.broadcasted_iota(jnp.int32, (devices, angles), 1) // share
        packed = jnp.zeros((devices, angles), jnp.float32)
        for j in range(owned):
            out_ref[pl.ds(j, devices, stride=AUX), :] = grads_ref[
                pl.ds(j, devices, stride=owned), :
            ]
            mine = weights_ref[pl.ds(j, devices, stride=owned), :]
            packed = jnp.where(lane == j, mine, packed)
        out_ref[pl.ds(owned, devices, stride=AUX), :] = packed
        out_ref[pl.ds(owned + 1, devices, stride=AUX), :] = error_ref[...]
        for j in range(owned + 2, AUX):
            out_ref[pl.ds(j, devices, stride=AUX), :] = jnp.zeros((devices, angles), jnp.float32)


def class_sums(received, owned):
    devices, rows, angles = received.shape
    count = rows - AUX
    classes = owned * devices
    return pl.pallas_call(
        classes_kernel,
        out_shape=jax.ShapeDtypeStruct((devices * AUX, angles), jnp.float32),
        grid=(devices // SOURCES,),
        in_specs=[
            pl.BlockSpec((SOURCES, count, angles), lambda i: (i, 0, 0)),
            pl.BlockSpec((devices, AUX, angles), lambda i: (0, count // AUX, 0)),
        ],
        out_specs=pl.BlockSpec((devices * AUX, angles), lambda i: (0, 0)),
        scratch_shapes=[
            pltpu.VMEM((devices * AUX, angles), jnp.float32),
            pltpu.VMEM((devices, count), jnp.float32),
            pltpu.VMEM((devices, count), jnp.float32),
            pltpu.VMEM((classes, angles), jnp.float32),
            pltpu.VMEM((angles, classes), jnp.bfloat16),
            pltpu.VMEM((angles + TILE, classes), jnp.float32),
            pltpu.VMEM((classes, angles), jnp.float32),
            pltpu.VMEM((classes, angles), jnp.float32),
            pltpu.VMEM((devices, count), jnp.float32),
        ],
        compiler_params=pltpu.CompilerParams(
            dimension_semantics=("arbitrary",), vmem_limit_bytes=48 << 20
        ),
        name="class_sums",
    )(received, received)


def update_kernel(back_ref, averages_ref, velocity_ref, new_averages_ref, new_velocity_ref, error_ref):
    owned, grid_rows, angles = averages_ref.shape
    share = angles // owned
    packed = back_ref[pl.ds(owned, grid_rows, stride=AUX), :]
    for j in range(owned):
        grads = back_ref[pl.ds(j, grid_rows, stride=AUX), :]
        weights = jnp.broadcast_to(packed[:, j * share : j * share + 1], (grid_rows, angles))
        old = averages_ref[j]
        step = (grads - RIDGE * old) / (weights + RIDGE)
        moved = MOMENTUM * velocity_ref[j] + step
        new_velocity_ref[j] = moved
        new_averages_ref[j] = old + RATE * moved
    parts = back_ref[pl.ds(owned + 1, grid_rows, stride=AUX), :]
    error_ref[...] = jnp.sum(parts, axis=0, keepdims=True) / (grid_rows * angles)


def update(back, averages, velocity, count):
    owned = averages.shape[0]
    grid_rows, angles = 2 * averages.shape[2], averages.shape[3]
    flat = (owned, grid_rows, angles)
    new_averages, new_velocity, errors = pl.pallas_call(
        update_kernel,
        out_shape=(
            jax.ShapeDtypeStruct(flat, jnp.float32),
            jax.ShapeDtypeStruct(flat, jnp.float32),
            jax.ShapeDtypeStruct((1, count), jnp.float32),
        ),
        compiler_params=pltpu.CompilerParams(vmem_limit_bytes=48 << 20),
        name="update",
    )(back, averages.reshape(flat), velocity.reshape(flat))
    return (
        new_averages.reshape(averages.shape),
        new_velocity.reshape(averages.shape),
        errors.reshape(count),
    )


def on_device(stack, batch_index, best_class, best_rot, best_shift, ctf, averages, velocity):
    everyone = ("dom", "cls")
    sent = align(stack, batch_index, best_class, best_rot, best_shift, ctf, averages)
    received = lax.all_to_all(sent, everyone, split_axis=0, concat_axis=0, tiled=True)
    partial = class_sums(received, averages.shape[0])
    devices = received.shape[0]
    partial = partial.reshape(devices, AUX, received.shape[2])
    back = lax.all_to_all(partial, everyone, split_axis=0, concat_axis=0, tiled=True)
    back = back.reshape(devices * AUX, received.shape[2])
    return update(back, averages, velocity, batch_index.shape[0])


def solution(mesh):
    whole = ("dom", "cls")
    in_specs = (
        P(whole, None, None, None),
        P(whole),
        P(whole),
        P(whole),
        P(whole, None),
        P(whole, None),
        P(whole, None, None, None),
        P(whole, None, None, None),
    )
    out_specs = (P(whole, None, None, None), P(whole, None, None, None), P(whole))
    return jax.shard_map(
        on_device, mesh=mesh, in_specs=in_specs, out_specs=out_specs, check_vma=False
    )
```

```python
import numpy as np
import jax
import jax.numpy as jnp
from jax import lax
from jax.experimental import pallas as pl
from jax.experimental.pallas import tpu as pltpu
from jax.sharding import PartitionSpec as P

IMG = 128
TOP_SHIFT = 4
MOMENTUM = 0.9
RATE = 0.5
RIDGE = 1.0
BATCH = 16
SOURCES = 16
AUX = 8
PAD = 8
TILE = 16
HALF_CLASSES = 256


def phase_tables(cycles, angles):
    radius = np.arange(1, cycles + 1, dtype=np.float64)[:, None]
    theta = 2.0 * np.pi * np.arange(angles, dtype=np.float64)[None, :] / angles
    shifts = np.arange(-TOP_SHIFT, TOP_SHIFT + 1, dtype=np.float64)[:, None, None]
    tables = []
    for along in (np.cos(theta), np.sin(theta)):
        phase = 2.0 * np.pi * radius * along / IMG * shifts
        tables.append(np.stack([np.cos(phase), np.sin(phase)], axis=1))
    return np.stack(tables).astype(np.float32)


def align_kernel(
    index_hbm,
    rot_hbm,
    shift_hbm,
    stack_hbm,
    table_hbm,
    ctf_hbm,
    class_hbm,
    averages_hbm,
    out_ref,
    rows_ref,
    turned_ref,
    other_ref,
    table_ref,
    index_ref,
    rot_ref,
    shift_ref,
    ctf_ref,
    class_ref,
    averages_ref,
    row_sems,
    sems,
):
    cycles, angles = table_ref.shape[3], table_ref.shape[4]
    grid_rows = 2 * cycles
    count = rows_ref.shape[0]
    chunks = count // BATCH
    owned = averages_ref.shape[0]
    pitch = grid_rows + PAD
    pairs = (
        (index_hbm, index_ref),
        (table_hbm, table_ref),
        (rot_hbm, rot_ref),
        (shift_hbm, shift_ref),
        (ctf_hbm, ctf_ref),
        (class_hbm, class_ref),
        (averages_hbm, averages_ref),
    )
    copies = [pltpu.make_async_copy(a, b, sems.at[n]) for n, (a, b) in enumerate(pairs)]
    for copy in copies:
        copy.start()
    copies[0].wait()

    def issue(i, carry):
        for j in range(BATCH):
            pltpu.make_async_copy(
                stack_hbm.at[index_ref[i * BATCH + j]], rows_ref.at[i * BATCH + j], row_sems.at[i]
            ).start()
        return carry

    lax.fori_loop(0, chunks, issue, 0)
    for copy in copies[2:]:
        copy.wait()

    classes = (class_ref[...] - HALF_CLASSES).astype(jnp.float32)
    gamma = ctf_ref[...].astype(jnp.float32)
    turned_ref[0:grid_rows, :] = jnp.broadcast_to(classes, (grid_rows, angles))
    turned_ref[pitch : pitch + cycles, :] = gamma
    turned_ref[pitch + cycles : pitch + grid_rows, :] = gamma
    for j in range(owned):
        turned_ref[(2 + j) * pitch : (2 + j) * pitch + grid_rows, :] = averages_ref[j]
    for j in range(2 + owned, AUX):
        turned_ref[j * pitch : j * pitch + grid_rows, :] = jnp.zeros(
            (grid_rows, angles), jnp.float32
        )

    def spread_aux(r, carry):
        got = turned_ref[pl.ds(r, AUX, stride=pitch), :]
        out_ref[r, pl.ds(count, AUX), :] = got.astype(jnp.bfloat16)
        return carry

    lax.fori_loop(0, grid_rows, spread_aux, 0, unroll=32)
    copies[1].wait()

    def turn(i, turned):
        first = i * BATCH
        pltpu.make_async_copy(
            stack_hbm.at[pl.ds(0, BATCH)], rows_ref.at[pl.ds(first, BATCH)], row_sems.at[i]
        ).wait()
        for j in range(BATCH):
            particle = first + j
            sx = shift_ref[0, particle] + TOP_SHIFT
            sy = shift_ref[1, particle] + TOP_SHIFT
            back = (angles - 2 * rot_ref[particle]) % angles
            xr, xi = table_ref[0, sx, 0], table_ref[0, sx, 1]
            yr, yi = table_ref[1, sy, 0], table_ref[1, sy, 1]
            cosine = xr * yr - xi * yi
            sine = xr * yi + xi * yr
            real = rows_ref[particle, 0].astype(jnp.float32)
            imag = rows_ref[particle, 1].astype(jnp.float32)
            base = j * pitch
            turned[base : base + cycles, :] = pltpu.roll(cosine * real - sine * imag, back, 1)
            turned[base + cycles : base + grid_rows, :] = pltpu.roll(
                sine * real + cosine * imag, back, 1
            )

    def spread(i, turned):
        first = pl.multiple_of(i * BATCH, BATCH)
        for r in range(grid_rows):
            got = turned[pl.ds(r, BATCH, stride=pitch), :]
            out_ref[r, pl.ds(first, BATCH), :] = got.astype(jnp.bfloat16)

    turn(0, turned_ref)

    def two(h, carry):
        turn(2 * h + 1, other_ref)
        spread(2 * h, turned_ref)
        turn(2 * h + 2, turned_ref)
        spread(2 * h + 1, other_ref)
        return carry

    lax.fori_loop(0, chunks // 2 - 1, two, 0)
    turn(chunks - 1, other_ref)
    spread(chunks - 2, turned_ref)
    spread(chunks - 1, other_ref)


def align(stack, batch_index, best_class, best_rot, best_shift, ctf, averages):
    count = batch_index.shape[0]
    cycles, angles = stack.shape[2], stack.shape[3]
    grid_rows = 2 * cycles
    owned = averages.shape[0]
    table = jnp.asarray(phase_tables(cycles, angles))
    operands = (
        batch_index,
        best_rot,
        best_shift.T,
        stack,
        table,
        ctf.T,
        best_class.reshape(1, count),
        averages.reshape(owned, grid_rows, angles),
    )
    return pl.pallas_call(
        align_kernel,
        out_shape=jax.ShapeDtypeStruct((grid_rows, count + AUX, angles), jnp.bfloat16),
        in_specs=[pl.BlockSpec(memory_space=pltpu.HBM)] * len(operands),
        out_specs=pl.BlockSpec(memory_space=pltpu.VMEM),
        scratch_shapes=[
            pltpu.VMEM((count, 2, cycles, angles), jnp.bfloat16),
            pltpu.VMEM((BATCH * (grid_rows + PAD), angles), jnp.float32),
            pltpu.VMEM((BATCH * (grid_rows + PAD), angles), jnp.float32),
            pltpu.VMEM(table.shape, jnp.float32),
            pltpu.SMEM((count,), jnp.int32),
            pltpu.SMEM((count,), jnp.int32),
            pltpu.SMEM((2, count), jnp.int32),
            pltpu.VMEM((cycles, count), jnp.bfloat16),
            pltpu.VMEM((1, count), jnp.int32),
            pltpu.VMEM((owned, grid_rows, angles), jnp.float32),
            pltpu.SemaphoreType.DMA((count // BATCH,)),
            pltpu.SemaphoreType.DMA((7,)),
        ],
        compiler_params=pltpu.CompilerParams(vmem_limit_bytes=48 << 20),
        name="align",
    )(*[pltpu.with_memory_space_constraint(x, pltpu.HBM) for x in operands])


def classes_kernel(
    received_ref,
    out_ref,
    aux32_ref,
    class_ref,
    gamma_ref,
    model_ref,
    turned_model_ref,
    sums_ref,
    grads_ref,
    weights_ref,
    error_ref,
):
    devices, height, angles = received_ref.shape
    count = height - AUX
    classes = model_ref.shape[0]
    owned = classes // devices
    aux = received_ref[:, count:height, :]
    aux32_ref[...] = aux.astype(jnp.float32).reshape(devices * AUX, angles)
    class_ref[...] = aux32_ref[pl.ds(0, devices, stride=AUX), :]
    gamma_ref[...] = aux32_ref[pl.ds(1, devices, stride=AUX), :]
    for j in range(owned):
        model_ref[pl.ds(j, devices, stride=owned), :] = aux32_ref[
            pl.ds(2 + j, devices, stride=AUX), :
        ]
    turned_model_ref[...] = model_ref[...].T.astype(jnp.bfloat16)
    sums_ref[...] = jnp.zeros(sums_ref.shape, jnp.float32)

    def step(i, carry):
        first = pl.multiple_of(i * SOURCES, SOURCES)
        class_block = class_ref[pl.ds(first, SOURCES), :]
        gamma_block = gamma_ref[pl.ds(first, SOURCES), :]
        down = lax.broadcasted_iota(jnp.int32, (classes, count), 0) - HALF_CLASSES
        down = down.astype(jnp.float32).astype(jnp.bfloat16)
        zero = jnp.zeros((), jnp.bfloat16)
        last_dims = (((1,), (1,)), ((), ()))
        errors = []
        for pair in range(SOURCES // 2):
            tables = []
            gammas = []
            for b in (2 * pair, 2 * pair + 1):
                name = class_block[b : b + 1, :].astype(jnp.bfloat16)
                gamma = gamma_block[b : b + 1, :]
                tables.append(jnp.where(down == name, gamma.astype(jnp.bfloat16), zero))
                gammas.append(jnp.broadcast_to(gamma, (TILE, count)))
            table = jnp.concatenate(tables, axis=1)
            rows = received_ref[pl.ds(first + 2 * pair, 2), 0:count, :].reshape(2 * count, angles)
            turned = rows.astype(jnp.float32).T
            resid = turned - jnp.dot(
                turned_model_ref[...], table, preferred_element_type=jnp.float32
            )
            error = jnp.sum(resid * resid, axis=0, keepdims=True)
            errors += [error[:, 0:count], error[:, count : 2 * count]]
            values = jnp.concatenate([turned, jnp.concatenate(gammas, axis=1)], axis=0)
            sums_ref[...] += lax.dot_general(
                values.astype(jnp.bfloat16), table, last_dims, preferred_element_type=jnp.float32
            )
        error_ref[pl.ds(first, SOURCES), :] = jnp.concatenate(errors, axis=0)
        return carry

    lax.fori_loop(0, devices // SOURCES, step, 0)

    weights = jnp.broadcast_to(sums_ref[angles : angles + 1, :], (angles, classes)).T
    weights_ref[...] = weights
    grads_ref[...] = sums_ref[0:angles, :].T - weights * model_ref[...]
    share = angles // owned
    lane = lax.broadcasted_iota(jnp.int32, (devices, angles), 1) // share
    packed = jnp.zeros((devices, angles), jnp.float32)
    back = owned + 2
    for j in range(owned):
        out_ref[pl.ds(j, devices, stride=back), :] = grads_ref[pl.ds(j, devices, stride=owned), :]
        packed = jnp.where(lane == j, weights_ref[pl.ds(j, devices, stride=owned), :], packed)
    out_ref[pl.ds(owned, devices, stride=back), :] = packed
    out_ref[pl.ds(owned + 1, devices, stride=back), :] = error_ref[...]


def class_sums(received, owned):
    devices, height, angles = received.shape
    count = height - AUX
    classes = owned * devices
    return pl.pallas_call(
        classes_kernel,
        out_shape=jax.ShapeDtypeStruct((devices * (owned + 2), angles), jnp.float32),
        in_specs=[pl.BlockSpec(memory_space=pltpu.VMEM)],
        out_specs=pl.BlockSpec(memory_space=pltpu.VMEM),
        scratch_shapes=[
            pltpu.VMEM((devices * AUX, angles), jnp.float32),
            pltpu.VMEM((devices, count), jnp.float32),
            pltpu.VMEM((devices, count), jnp.float32),
            pltpu.VMEM((classes, angles), jnp.float32),
            pltpu.VMEM((angles, classes), jnp.bfloat16),
            pltpu.VMEM((angles + TILE, classes), jnp.float32),
            pltpu.VMEM((classes, angles), jnp.float32),
            pltpu.VMEM((classes, angles), jnp.float32),
            pltpu.VMEM((devices, count), jnp.float32),
        ],
        compiler_params=pltpu.CompilerParams(vmem_limit_bytes=48 << 20),
        name="class_sums",
    )(received)


def update_kernel(back_ref, averages_ref, velocity_ref, new_averages_ref, new_velocity_ref, error_ref):
    owned, grid_rows, angles = averages_ref.shape
    share = angles // owned
    pitch = owned + 2
    packed = back_ref[pl.ds(owned, grid_rows, stride=pitch), :]
    for j in range(owned):
        grads = back_ref[pl.ds(j, grid_rows, stride=pitch), :]
        weights = jnp.broadcast_to(packed[:, j * share : j * share + 1], (grid_rows, angles))
        old = averages_ref[j]
        step = (grads - RIDGE * old) / (weights + RIDGE)
        moved = MOMENTUM * velocity_ref[j] + step
        new_velocity_ref[j] = moved
        new_averages_ref[j] = old + RATE * moved
    parts = back_ref[pl.ds(owned + 1, grid_rows, stride=pitch), :]
    error_ref[...] = jnp.sum(parts, axis=0, keepdims=True) / (grid_rows * angles)


def update(back, averages, velocity, count):
    owned = averages.shape[0]
    grid_rows, angles = 2 * averages.shape[2], averages.shape[3]
    flat = (owned, grid_rows, angles)
    new_averages, new_velocity, errors = pl.pallas_call(
        update_kernel,
        out_shape=(
            jax.ShapeDtypeStruct(flat, jnp.float32),
            jax.ShapeDtypeStruct(flat, jnp.float32),
            jax.ShapeDtypeStruct((1, count), jnp.float32),
        ),
        compiler_params=pltpu.CompilerParams(vmem_limit_bytes=48 << 20),
        name="update",
    )(back, averages.reshape(flat), velocity.reshape(flat))
    return (
        new_averages.reshape(averages.shape),
        new_velocity.reshape(averages.shape),
        errors.reshape(count),
    )


def on_device(stack, batch_index, best_class, best_rot, best_shift, ctf, averages, velocity):
    everyone = ("dom", "cls")
    sent = align(stack, batch_index, best_class, best_rot, best_shift, ctf, averages)
    received = lax.all_to_all(sent, everyone, split_axis=0, concat_axis=0, tiled=True)
    partial = class_sums(received, averages.shape[0])
    height, angles = partial.shape
    partial = partial.reshape(height // 2, 2, angles)
    back = lax.all_to_all(partial, everyone, split_axis=0, concat_axis=0, tiled=True)
    back = back.reshape(height, angles)
    return update(back, averages, velocity, batch_index.shape[0])


def solution(mesh):
    whole = ("dom", "cls")
    in_specs = (
        P(whole, None, None, None),
        P(whole),
        P(whole),
        P(whole),
        P(whole, None),
        P(whole, None),
        P(whole, None, None, None),
        P(whole, None, None, None),
    )
    out_specs = (P(whole, None, None, None), P(whole, None, None, None), P(whole))
    return jax.shard_map(
        on_device, mesh=mesh, in_specs=in_specs, out_specs=out_specs, check_vma=False
    )
```

```python
import numpy as np
import jax
import jax.numpy as jnp
from jax import lax
from jax.experimental import pallas as pl
from jax.experimental.pallas import tpu as pltpu
from jax.sharding import PartitionSpec as P

IMG = 128
TOP_SHIFT = 4
MOMENTUM = 0.9
RATE = 0.5
RIDGE = 1.0
BATCH = 16
SOURCES = 16
AUX = 8
PAD = 8
SPARE = 8
HALF_CLASSES = 256


def phase_tables(cycles, angles):
    radius = np.arange(1, cycles + 1, dtype=np.float64)[:, None]
    theta = 2.0 * np.pi * np.arange(angles, dtype=np.float64)[None, :] / angles
    shifts = np.arange(-TOP_SHIFT, TOP_SHIFT + 1, dtype=np.float64)[:, None, None]
    tables = []
    for along in (np.cos(theta), np.sin(theta)):
        phase = 2.0 * np.pi * radius * along / IMG * shifts
        tables.append(np.stack([np.cos(phase), np.sin(phase)], axis=1))
    return np.stack(tables).astype(np.float32)


def align_kernel(
    index_hbm,
    rot_hbm,
    shift_hbm,
    stack_hbm,
    table_hbm,
    ctf_hbm,
    class_hbm,
    averages_hbm,
    out_ref,
    rows_ref,
    turned_ref,
    other_ref,
    table_ref,
    index_ref,
    rot_ref,
    shift_ref,
    ctf_ref,
    class_ref,
    averages_ref,
    row_sems,
    sems,
):
    cycles, angles = table_ref.shape[3], table_ref.shape[4]
    grid_rows = 2 * cycles
    count = rows_ref.shape[0]
    chunks = count // BATCH
    owned = averages_ref.shape[0]
    pitch = grid_rows + PAD
    pairs = (
        (index_hbm, index_ref),
        (table_hbm, table_ref),
        (rot_hbm, rot_ref),
        (shift_hbm, shift_ref),
        (ctf_hbm, ctf_ref),
        (class_hbm, class_ref),
        (averages_hbm, averages_ref),
    )
    copies = [pltpu.make_async_copy(a, b, sems.at[n]) for n, (a, b) in enumerate(pairs)]
    for copy in copies:
        copy.start()
    copies[0].wait()

    def issue(i):
        for j in range(BATCH):
            pltpu.make_async_copy(
                stack_hbm.at[index_ref[i * BATCH + j]], rows_ref.at[i * BATCH + j], row_sems.at[i]
            ).start()

    issue(0)
    issue(1)
    for copy in copies[2:]:
        copy.wait()

    classes = (class_ref[...] - HALF_CLASSES).astype(jnp.float32)
    gamma = ctf_ref[...].astype(jnp.float32)
    turned_ref[0:grid_rows, :] = jnp.broadcast_to(classes, (grid_rows, angles))
    turned_ref[pitch : pitch + cycles, :] = gamma
    turned_ref[pitch + cycles : pitch + grid_rows, :] = gamma
    for j in range(owned):
        turned_ref[(2 + j) * pitch : (2 + j) * pitch + grid_rows, :] = averages_ref[j]
    for j in range(2 + owned, AUX):
        turned_ref[j * pitch : j * pitch + grid_rows, :] = jnp.zeros(
            (grid_rows, angles), jnp.float32
        )

    def spread_aux(r, carry):
        got = turned_ref[pl.ds(r, AUX, stride=pitch), :]
        out_ref[r, pl.ds(count, AUX), :] = got.astype(jnp.bfloat16)
        return carry

    lax.fori_loop(0, grid_rows, spread_aux, 0, unroll=32)
    copies[1].wait()

    def turn(i, turned):
        first = i * BATCH
        if i + 2 < chunks:
            issue(i + 2)
        pltpu.make_async_copy(
            stack_hbm.at[pl.ds(0, BATCH)], rows_ref.at[pl.ds(first, BATCH)], row_sems.at[i]
        ).wait()
        for j in range(BATCH):
            particle = first + j
            sx = shift_ref[0, particle] + TOP_SHIFT
            sy = shift_ref[1, particle] + TOP_SHIFT
            back = (angles - 2 * rot_ref[particle]) % angles
            xr, xi = table_ref[0, sx, 0], table_ref[0, sx, 1]
            yr, yi = table_ref[1, sy, 0], table_ref[1, sy, 1]
            cosine = xr * yr - xi * yi
            sine = xr * yi + xi * yr
            real = rows_ref[particle, 0].astype(jnp.float32)
            imag = rows_ref[particle, 1].astype(jnp.float32)
            base = j * pitch
            turned[base : base + cycles, :] = pltpu.roll(cosine * real - sine * imag, back, 1)
            turned[base + cycles : base + grid_rows, :] = pltpu.roll(
                sine * real + cosine * imag, back, 1
            )

    def spread(i, turned):
        first = i * BATCH
        for r in range(grid_rows):
            got = turned[pl.ds(r, BATCH, stride=pitch), :]
            out_ref[r, pl.ds(first, BATCH), :] = got.astype(jnp.bfloat16)

    scratches = (turned_ref, other_ref)
    turn(0, scratches[0])
    for i in range(1, chunks):
        turn(i, scratches[i % 2])
        spread(i - 1, scratches[(i - 1) % 2])
    spread(chunks - 1, scratches[(chunks - 1) % 2])


def align(stack, batch_index, best_class, best_rot, best_shift, ctf, averages):
    count = batch_index.shape[0]
    cycles, angles = stack.shape[2], stack.shape[3]
    grid_rows = 2 * cycles
    owned = averages.shape[0]
    table = jnp.asarray(phase_tables(cycles, angles))
    operands = (
        batch_index,
        best_rot,
        best_shift.T,
        stack,
        table,
        ctf.T,
        best_class.reshape(1, count),
        averages.reshape(owned, grid_rows, angles),
    )
    return pl.pallas_call(
        align_kernel,
        out_shape=jax.ShapeDtypeStruct((grid_rows, count + AUX, angles), jnp.bfloat16),
        in_specs=[pl.BlockSpec(memory_space=pltpu.HBM)] * len(operands),
        out_specs=pl.BlockSpec(memory_space=pltpu.VMEM),
        scratch_shapes=[
            pltpu.VMEM((count, 2, cycles, angles), jnp.bfloat16),
            pltpu.VMEM((BATCH * (grid_rows + PAD), angles), jnp.float32),
            pltpu.VMEM((BATCH * (grid_rows + PAD), angles), jnp.float32),
            pltpu.VMEM(table.shape, jnp.float32),
            pltpu.SMEM((count,), jnp.int32),
            pltpu.SMEM((count,), jnp.int32),
            pltpu.SMEM((2, count), jnp.int32),
            pltpu.VMEM((cycles, count), jnp.bfloat16),
            pltpu.VMEM((1, count), jnp.int32),
            pltpu.VMEM((owned, grid_rows, angles), jnp.float32),
            pltpu.SemaphoreType.DMA((count // BATCH,)),
            pltpu.SemaphoreType.DMA((7,)),
        ],
        compiler_params=pltpu.CompilerParams(vmem_limit_bytes=48 << 20),
        name="align",
    )(*[pltpu.with_memory_space_constraint(x, pltpu.HBM) for x in operands])


def classes_kernel(
    received_ref,
    out_ref,
    aux32_ref,
    class_ref,
    gamma_ref,
    model_ref,
    turned_model_ref,
    sums_ref,
    grads_ref,
    weights_ref,
    error_ref,
    table_ref,
):
    devices, height, angles = received_ref.shape
    count = height - AUX
    classes = model_ref.shape[0]
    owned = classes // devices
    aux = received_ref[:, count:height, :]
    aux32_ref[...] = aux.astype(jnp.float32).reshape(devices * AUX, angles)
    class_ref[...] = aux32_ref[pl.ds(0, devices, stride=AUX), :]
    gamma_ref[...] = aux32_ref[pl.ds(1, devices, stride=AUX), :]
    for j in range(owned):
        model_ref[pl.ds(j, devices, stride=owned), :] = aux32_ref[
            pl.ds(2 + j, devices, stride=AUX), :
        ]
    turned_model_ref[...] = model_ref[...].T.astype(jnp.bfloat16)
    sums_ref[...] = jnp.zeros(sums_ref.shape, jnp.float32)

    def step(i, carry):
        first = pl.multiple_of(i * SOURCES, SOURCES)
        class_block = class_ref[pl.ds(first, SOURCES), :]
        gamma_block = gamma_ref[pl.ds(first, SOURCES), :]
        down = lax.broadcasted_iota(jnp.int32, (classes, count), 0) - HALF_CLASSES
        down = down.astype(jnp.float32).astype(jnp.bfloat16)
        zero = jnp.zeros((), jnp.bfloat16)
        errors = []
        for pair in range(SOURCES // 2):
            tables = []
            for b in (2 * pair, 2 * pair + 1):
                name = class_block[b : b + 1, :].astype(jnp.bfloat16)
                gamma = gamma_block[b : b + 1, :]
                tables.append(jnp.where(down == name, gamma.astype(jnp.bfloat16), zero))
            table = jnp.concatenate(tables, axis=1)
            rows = received_ref[pl.ds(first + 2 * pair, 2), 0:count, :].reshape(2 * count, angles)
            turned = rows.astype(jnp.float32).T
            resid = turned - jnp.dot(
                turned_model_ref[...], table, preferred_element_type=jnp.float32
            )
            error = jnp.sum(resid * resid, axis=0, keepdims=True)
            errors += [error[:, 0:count], error[:, count : 2 * count]]
            table_ref[:, 2 * pair * count : 2 * (pair + 1) * count] = table
        columns = [
            jnp.broadcast_to(gamma_block[b : b + 1, :], (SPARE, count)).T for b in range(SOURCES)
        ]
        rows = received_ref[pl.ds(first, SOURCES), 0:count, :].reshape(SOURCES * count, angles)
        columns = jnp.concatenate(columns, axis=0).astype(jnp.bfloat16)
        sums_ref[...] += jnp.dot(
            table_ref[...],
            jnp.concatenate([rows, columns], axis=1),
            preferred_element_type=jnp.float32,
        )
        error_ref[pl.ds(first, SOURCES), :] = jnp.concatenate(errors, axis=0)
        return carry

    lax.fori_loop(0, devices // SOURCES, step, 0, unroll=8)

    weights = jnp.broadcast_to(sums_ref[:, angles : angles + 1], (classes, angles))
    weights_ref[...] = weights
    grads_ref[...] = sums_ref[:, 0:angles] - weights * model_ref[...]
    share = angles // owned
    lane = lax.broadcasted_iota(jnp.int32, (devices, angles), 1) // share
    packed = jnp.zeros((devices, angles), jnp.float32)
    back = owned + 2
    for j in range(owned):
        out_ref[pl.ds(j, devices, stride=back), :] = grads_ref[pl.ds(j, devices, stride=owned), :]
        packed = jnp.where(lane == j, weights_ref[pl.ds(j, devices, stride=owned), :], packed)
    out_ref[pl.ds(owned, devices, stride=back), :] = packed
    out_ref[pl.ds(owned + 1, devices, stride=back), :] = error_ref[...]


def class_sums(received, owned):
    devices, height, angles = received.shape
    count = height - AUX
    classes = owned * devices
    return pl.pallas_call(
        classes_kernel,
        out_shape=jax.ShapeDtypeStruct((devices * (owned + 2), angles), jnp.float32),
        in_specs=[pl.BlockSpec(memory_space=pltpu.VMEM)],
        out_specs=pl.BlockSpec(memory_space=pltpu.VMEM),
        scratch_shapes=[
            pltpu.VMEM((devices * AUX, angles), jnp.float32),
            pltpu.VMEM((devices, count), jnp.float32),
            pltpu.VMEM((devices, count), jnp.float32),
            pltpu.VMEM((classes, angles), jnp.float32),
            pltpu.VMEM((angles, classes), jnp.bfloat16),
            pltpu.VMEM((classes, angles + SPARE), jnp.float32),
            pltpu.VMEM((classes, angles), jnp.float32),
            pltpu.VMEM((classes, angles), jnp.float32),
            pltpu.VMEM((devices, count), jnp.float32),
            pltpu.VMEM((classes, SOURCES * count), jnp.bfloat16),
        ],
        compiler_params=pltpu.CompilerParams(vmem_limit_bytes=48 << 20),
        name="class_sums",
    )(received)


def update_kernel(back_ref, averages_ref, velocity_ref, new_averages_ref, new_velocity_ref, error_ref):
    owned, grid_rows, angles = averages_ref.shape
    share = angles // owned
    pitch = owned + 2
    packed = back_ref[pl.ds(owned, grid_rows, stride=pitch), :]
    for j in range(owned):
        grads = back_ref[pl.ds(j, grid_rows, stride=pitch), :]
        weights = jnp.broadcast_to(packed[:, j * share : j * share + 1], (grid_rows, angles))
        old = averages_ref[j]
        step = (grads - RIDGE * old) / (weights + RIDGE)
        moved = MOMENTUM * velocity_ref[j] + step
        new_velocity_ref[j] = moved
        new_averages_ref[j] = old + RATE * moved
    parts = back_ref[pl.ds(owned + 1, grid_rows, stride=pitch), :]
    error_ref[...] = jnp.sum(parts, axis=0, keepdims=True) / (grid_rows * angles)


def update(back, averages, velocity, count):
    owned = averages.shape[0]
    grid_rows, angles = 2 * averages.shape[2], averages.shape[3]
    flat = (owned, grid_rows, angles)
    new_averages, new_velocity, errors = pl.pallas_call(
        update_kernel,
        out_shape=(
            jax.ShapeDtypeStruct(flat, jnp.float32),
            jax.ShapeDtypeStruct(flat, jnp.float32),
            jax.ShapeDtypeStruct((1, count), jnp.float32),
        ),
        compiler_params=pltpu.CompilerParams(vmem_limit_bytes=48 << 20),
        name="update",
    )(back, averages.reshape(flat), velocity.reshape(flat))
    return (
        new_averages.reshape(averages.shape),
        new_velocity.reshape(averages.shape),
        errors.reshape(count),
    )


def on_device(stack, batch_index, best_class, best_rot, best_shift, ctf, averages, velocity):
    everyone = ("dom", "cls")
    sent = align(stack, batch_index, best_class, best_rot, best_shift, ctf, averages)
    received = lax.all_to_all(sent, everyone, split_axis=0, concat_axis=0, tiled=True)
    partial = class_sums(received, averages.shape[0])
    height, angles = partial.shape
    partial = partial.reshape(height // 2, 2, angles)
    back = lax.all_to_all(partial, everyone, split_axis=0, concat_axis=0, tiled=True)
    back = back.reshape(height, angles)
    return update(back, averages, velocity, batch_index.shape[0])


def solution(mesh):
    whole = ("dom", "cls")
    in_specs = (
        P(whole, None, None, None),
        P(whole),
        P(whole),
        P(whole),
        P(whole, None),
        P(whole, None),
        P(whole, None, None, None),
        P(whole, None, None, None),
    )
    out_specs = (P(whole, None, None, None), P(whole, None, None, None), P(whole))
    return jax.shard_map(
        on_device, mesh=mesh, in_specs=in_specs, out_specs=out_specs, check_vma=False
    )
```

```python
import numpy as np
import jax
import jax.numpy as jnp
from jax import lax
from jax.experimental import pallas as pl
from jax.experimental.pallas import tpu as pltpu
from jax.sharding import PartitionSpec as P

IMG = 128
TOP_SHIFT = 4
MOMENTUM = 0.9
RATE = 0.5
RIDGE = 1.0
BATCH = 16
SOURCES = 16
AUX = 8
PAD = 8
SPARE = 8
HALF_CLASSES = 256


def phase_tables(cycles, angles):
    radius = np.arange(1, cycles + 1, dtype=np.float64)[:, None]
    theta = 2.0 * np.pi * np.arange(angles, dtype=np.float64)[None, :] / angles
    shifts = np.arange(-TOP_SHIFT, TOP_SHIFT + 1, dtype=np.float64)[:, None, None]
    tables = []
    for along in (np.cos(theta), np.sin(theta)):
        phase = 2.0 * np.pi * radius * along / IMG * shifts
        tables.append(np.stack([np.cos(phase), np.sin(phase)], axis=1))
    return np.stack(tables).astype(np.float32)


def align_kernel(
    index_hbm,
    rot_hbm,
    shift_hbm,
    stack_hbm,
    table_hbm,
    ctf_hbm,
    class_hbm,
    averages_hbm,
    out_ref,
    rows_ref,
    turned_ref,
    other_ref,
    table_ref,
    index_ref,
    rot_ref,
    shift_ref,
    ctf_ref,
    class_ref,
    averages_ref,
    row_sems,
    sems,
):
    cycles, angles = table_ref.shape[3], table_ref.shape[4]
    grid_rows = 2 * cycles
    count = rows_ref.shape[0]
    chunks = count // BATCH
    owned = averages_ref.shape[0]
    pitch = grid_rows + PAD
    pairs = (
        (index_hbm, index_ref),
        (table_hbm, table_ref),
        (rot_hbm, rot_ref),
        (shift_hbm, shift_ref),
        (ctf_hbm, ctf_ref),
        (class_hbm, class_ref),
        (averages_hbm, averages_ref),
    )
    copies = [pltpu.make_async_copy(a, b, sems.at[n]) for n, (a, b) in enumerate(pairs)]
    for copy in copies:
        copy.start()
    copies[0].wait()

    def issue(i):
        for j in range(BATCH):
            pltpu.make_async_copy(
                stack_hbm.at[index_ref[i * BATCH + j]], rows_ref.at[i * BATCH + j], row_sems.at[i]
            ).start()

    issue(0)
    issue(1)
    for copy in copies[2:]:
        copy.wait()

    classes = (class_ref[...] - HALF_CLASSES).astype(jnp.float32)
    gamma = ctf_ref[...].astype(jnp.float32)
    turned_ref[0:grid_rows, :] = jnp.broadcast_to(classes, (grid_rows, angles))
    turned_ref[pitch : pitch + cycles, :] = gamma
    turned_ref[pitch + cycles : pitch + grid_rows, :] = gamma
    for j in range(owned):
        turned_ref[(2 + j) * pitch : (2 + j) * pitch + grid_rows, :] = averages_ref[j]
    for j in range(2 + owned, AUX):
        turned_ref[j * pitch : j * pitch + grid_rows, :] = jnp.zeros(
            (grid_rows, angles), jnp.float32
        )

    def spread_aux(r, carry):
        got = turned_ref[pl.ds(r, AUX, stride=pitch), :]
        out_ref[r, pl.ds(count, AUX), :] = got.astype(jnp.bfloat16)
        return carry

    lax.fori_loop(0, grid_rows, spread_aux, 0, unroll=32)
    copies[1].wait()

    def turn(i, turned):
        first = i * BATCH
        if i + 2 < chunks:
            issue(i + 2)
        pltpu.make_async_copy(
            stack_hbm.at[pl.ds(0, BATCH)], rows_ref.at[pl.ds(first, BATCH)], row_sems.at[i]
        ).wait()
        for j in range(BATCH):
            particle = first + j
            sx = shift_ref[0, particle] + TOP_SHIFT
            sy = shift_ref[1, particle] + TOP_SHIFT
            back = (angles - 2 * rot_ref[particle]) % angles
            xr, xi = table_ref[0, sx, 0], table_ref[0, sx, 1]
            yr, yi = table_ref[1, sy, 0], table_ref[1, sy, 1]
            cosine = xr * yr - xi * yi
            sine = xr * yi + xi * yr
            real = rows_ref[particle, 0].astype(jnp.float32)
            imag = rows_ref[particle, 1].astype(jnp.float32)
            base = j * pitch
            turned[base : base + cycles, :] = pltpu.roll(cosine * real - sine * imag, back, 1)
            turned[base + cycles : base + grid_rows, :] = pltpu.roll(
                sine * real + cosine * imag, back, 1
            )

    def spread(i, turned):
        first = i * BATCH
        for r in range(grid_rows):
            got = turned[pl.ds(r, BATCH, stride=pitch), :]
            out_ref[r, pl.ds(first, BATCH), :] = got.astype(jnp.bfloat16)

    scratches = (turned_ref, other_ref)
    turn(0, scratches[0])
    for i in range(1, chunks):
        turn(i, scratches[i % 2])
        spread(i - 1, scratches[(i - 1) % 2])
    spread(chunks - 1, scratches[(chunks - 1) % 2])


def align(stack, batch_index, best_class, best_rot, best_shift, ctf, averages):
    count = batch_index.shape[0]
    cycles, angles = stack.shape[2], stack.shape[3]
    grid_rows = 2 * cycles
    owned = averages.shape[0]
    table = jnp.asarray(phase_tables(cycles, angles))
    operands = (
        batch_index,
        best_rot,
        best_shift.T,
        stack,
        table,
        ctf.T,
        best_class.reshape(1, count),
        averages.reshape(owned, grid_rows, angles),
    )
    return pl.pallas_call(
        align_kernel,
        out_shape=jax.ShapeDtypeStruct((grid_rows, count + AUX, angles), jnp.bfloat16),
        in_specs=[pl.BlockSpec(memory_space=pltpu.HBM)] * len(operands),
        out_specs=pl.BlockSpec(memory_space=pltpu.VMEM),
        scratch_shapes=[
            pltpu.VMEM((count, 2, cycles, angles), jnp.bfloat16),
            pltpu.VMEM((BATCH * (grid_rows + PAD), angles), jnp.float32),
            pltpu.VMEM((BATCH * (grid_rows + PAD), angles), jnp.float32),
            pltpu.VMEM(table.shape, jnp.float32),
            pltpu.SMEM((count,), jnp.int32),
            pltpu.SMEM((count,), jnp.int32),
            pltpu.SMEM((2, count), jnp.int32),
            pltpu.VMEM((cycles, count), jnp.bfloat16),
            pltpu.VMEM((1, count), jnp.int32),
            pltpu.VMEM((owned, grid_rows, angles), jnp.float32),
            pltpu.SemaphoreType.DMA((count // BATCH,)),
            pltpu.SemaphoreType.DMA((7,)),
        ],
        compiler_params=pltpu.CompilerParams(vmem_limit_bytes=48 << 20),
        name="align",
    )(*[pltpu.with_memory_space_constraint(x, pltpu.HBM) for x in operands])


def classes_kernel(
    received_ref,
    out_ref,
    aux32_ref,
    class_ref,
    gamma_ref,
    model_ref,
    turned_model_ref,
    sums_ref,
    grads_ref,
    weights_ref,
    error_ref,
    table_ref,
    back_ref,
):
    devices, height, angles = received_ref.shape
    count = height - AUX
    classes = model_ref.shape[0]
    owned = classes // devices
    aux = received_ref[:, count:height, :]
    aux32_ref[...] = aux.astype(jnp.float32).reshape(devices * AUX, angles)
    class_ref[...] = aux32_ref[pl.ds(0, devices, stride=AUX), :]
    gamma_ref[...] = aux32_ref[pl.ds(1, devices, stride=AUX), :]
    for j in range(owned):
        model_ref[pl.ds(j, devices, stride=owned), :] = aux32_ref[
            pl.ds(2 + j, devices, stride=AUX), :
        ]
    turned_model_ref[...] = model_ref[...].T.astype(jnp.bfloat16)
    sums_ref[...] = jnp.zeros(sums_ref.shape, jnp.float32)

    def step(i, carry):
        first = pl.multiple_of(i * SOURCES, SOURCES)
        class_block = class_ref[pl.ds(first, SOURCES), :]
        gamma_block = gamma_ref[pl.ds(first, SOURCES), :]
        down = lax.broadcasted_iota(jnp.int32, (classes, count), 0) - HALF_CLASSES
        down = down.astype(jnp.float32).astype(jnp.bfloat16)
        zero = jnp.zeros((), jnp.bfloat16)
        errors = []
        for pair in range(SOURCES // 2):
            tables = []
            for b in (2 * pair, 2 * pair + 1):
                name = class_block[b : b + 1, :].astype(jnp.bfloat16)
                gamma = gamma_block[b : b + 1, :]
                tables.append(jnp.where(down == name, gamma.astype(jnp.bfloat16), zero))
            table = jnp.concatenate(tables, axis=1)
            rows = received_ref[pl.ds(first + 2 * pair, 2), 0:count, :].reshape(2 * count, angles)
            turned = rows.astype(jnp.float32).T
            resid = turned - jnp.dot(
                turned_model_ref[...], table, preferred_element_type=jnp.float32
            )
            error = jnp.sum(resid * resid, axis=0, keepdims=True)
            errors += [error[:, 0:count], error[:, count : 2 * count]]
            table_ref[:, 2 * pair * count : 2 * (pair + 1) * count] = table
        columns = [
            jnp.broadcast_to(gamma_block[b : b + 1, :], (SPARE, count)).T for b in range(SOURCES)
        ]
        rows = received_ref[pl.ds(first, SOURCES), 0:count, :].reshape(SOURCES * count, angles)
        columns = jnp.concatenate(columns, axis=0).astype(jnp.bfloat16)
        sums_ref[...] += jnp.dot(
            table_ref[...],
            jnp.concatenate([rows, columns], axis=1),
            preferred_element_type=jnp.float32,
        )
        error_ref[pl.ds(first, SOURCES), :] = jnp.concatenate(errors, axis=0)
        return carry

    lax.fori_loop(0, devices // SOURCES, step, 0, unroll=8)

    weights = jnp.broadcast_to(sums_ref[:, angles : angles + 1], (classes, angles))
    sums = sums_ref[:, 0:angles]
    grads = sums - weights * model_ref[...]
    raw = jnp.sum(sums * sums, axis=1, keepdims=True) < jnp.sum(
        grads * grads, axis=1, keepdims=True
    )
    raw = jnp.broadcast_to(raw.astype(jnp.float32), (classes, angles))
    grads_ref[...] = jnp.where(raw > 0.5, sums, grads)
    share = angles // owned
    part = lax.broadcasted_iota(jnp.int32, (classes, angles), 1) % share // (share // 4)
    high = weights.astype(jnp.bfloat16).astype(jnp.float32)
    weights_ref[...] = jnp.where(part == 0, high, jnp.where(part == 1, weights - high, raw))
    lane = lax.broadcasted_iota(jnp.int32, (devices, angles), 1) // share
    packed = jnp.zeros((devices, angles), jnp.float32)
    back = owned + 2
    for j in range(owned):
        back_ref[pl.ds(j, devices, stride=back), :] = grads_ref[pl.ds(j, devices, stride=owned), :]
        packed = jnp.where(lane == j, weights_ref[pl.ds(j, devices, stride=owned), :], packed)
    back_ref[pl.ds(owned, devices, stride=back), :] = packed
    back_ref[pl.ds(owned + 1, devices, stride=back), :] = error_ref[...]
    out_ref[...] = back_ref[...].astype(jnp.bfloat16)


def class_sums(received, owned):
    devices, height, angles = received.shape
    count = height - AUX
    classes = owned * devices
    return pl.pallas_call(
        classes_kernel,
        out_shape=jax.ShapeDtypeStruct((devices * (owned + 2), angles), jnp.bfloat16),
        in_specs=[pl.BlockSpec(memory_space=pltpu.VMEM)],
        out_specs=pl.BlockSpec(memory_space=pltpu.VMEM),
        scratch_shapes=[
            pltpu.VMEM((devices * AUX, angles), jnp.float32),
            pltpu.VMEM((devices, count), jnp.float32),
            pltpu.VMEM((devices, count), jnp.float32),
            pltpu.VMEM((classes, angles), jnp.float32),
            pltpu.VMEM((angles, classes), jnp.bfloat16),
            pltpu.VMEM((classes, angles + SPARE), jnp.float32),
            pltpu.VMEM((classes, angles), jnp.float32),
            pltpu.VMEM((classes, angles), jnp.float32),
            pltpu.VMEM((devices, count), jnp.float32),
            pltpu.VMEM((classes, SOURCES * count), jnp.bfloat16),
            pltpu.VMEM((devices * (owned + 2), angles), jnp.float32),
        ],
        compiler_params=pltpu.CompilerParams(vmem_limit_bytes=48 << 20),
        name="class_sums",
    )(received)


def update_kernel(
    sent_ref,
    averages_ref,
    velocity_ref,
    new_averages_ref,
    new_velocity_ref,
    error_ref,
    back_ref,
):
    owned, grid_rows, angles = averages_ref.shape
    share = angles // owned
    pitch = owned + 2
    back_ref[...] = sent_ref[...].astype(jnp.float32)
    packed = back_ref[pl.ds(owned, grid_rows, stride=pitch), :]
    for j in range(owned):
        base = j * share
        high = packed[:, base : base + 1]
        low = packed[:, base + share // 4 : base + share // 4 + 1]
        raw = packed[:, base + share // 2 : base + share // 2 + 1]
        weights = jnp.broadcast_to(high + low, (grid_rows, angles))
        old = averages_ref[j]
        model = old.astype(jnp.bfloat16).astype(jnp.float32)
        sent = back_ref[pl.ds(j, grid_rows, stride=pitch), :]
        grads = sent - jnp.broadcast_to(raw * (high + low), (grid_rows, angles)) * model
        step = (grads - RIDGE * old) / (weights + RIDGE)
        moved = MOMENTUM * velocity_ref[j] + step
        new_velocity_ref[j] = moved
        new_averages_ref[j] = old + RATE * moved
    parts = back_ref[pl.ds(owned + 1, grid_rows, stride=pitch), :]
    error_ref[...] = jnp.sum(parts, axis=0, keepdims=True) / (grid_rows * angles)


def update(back, averages, velocity, count):
    owned = averages.shape[0]
    grid_rows, angles = 2 * averages.shape[2], averages.shape[3]
    flat = (owned, grid_rows, angles)
    new_averages, new_velocity, errors = pl.pallas_call(
        update_kernel,
        out_shape=(
            jax.ShapeDtypeStruct(flat, jnp.float32),
            jax.ShapeDtypeStruct(flat, jnp.float32),
            jax.ShapeDtypeStruct((1, count), jnp.float32),
        ),
        scratch_shapes=[pltpu.VMEM(back.shape, jnp.float32)],
        compiler_params=pltpu.CompilerParams(vmem_limit_bytes=48 << 20),
        name="update",
    )(back, averages.reshape(flat), velocity.reshape(flat))
    return (
        new_averages.reshape(averages.shape),
        new_velocity.reshape(averages.shape),
        errors.reshape(count),
    )


def on_device(stack, batch_index, best_class, best_rot, best_shift, ctf, averages, velocity):
    everyone = ("dom", "cls")
    sent = align(stack, batch_index, best_class, best_rot, best_shift, ctf, averages)
    received = lax.all_to_all(sent, everyone, split_axis=0, concat_axis=0, tiled=True)
    partial = class_sums(received, averages.shape[0])
    height, angles = partial.shape
    partial = partial.reshape(height // 2, 2, angles)
    back = lax.all_to_all(partial, everyone, split_axis=0, concat_axis=0, tiled=True)
    back = back.reshape(height, angles)
    return update(back, averages, velocity, batch_index.shape[0])


def solution(mesh):
    whole = ("dom", "cls")
    in_specs = (
        P(whole, None, None, None),
        P(whole),
        P(whole),
        P(whole),
        P(whole, None),
        P(whole, None),
        P(whole, None, None, None),
        P(whole, None, None, None),
    )
    out_specs = (P(whole, None, None, None), P(whole, None, None, None), P(whole))
    return jax.shard_map(
        on_device, mesh=mesh, in_specs=in_specs, out_specs=out_specs, check_vma=False
    )
```

```python
import numpy as np
import jax
import jax.numpy as jnp
from jax import lax
from jax.experimental import pallas as pl
from jax.experimental.pallas import tpu as pltpu
from jax.sharding import PartitionSpec as P

IMG = 128
TOP_SHIFT = 4
MOMENTUM = 0.9
RATE = 0.5
RIDGE = 1.0
BATCH = 16
SOURCES = 16
AUX = 8
PAD = 8
SPARE = 8
HALF_CLASSES = 256


def phase_tables(cycles, angles):
    radius = np.arange(1, cycles + 1, dtype=np.float64)[:, None]
    theta = 2.0 * np.pi * np.arange(angles, dtype=np.float64)[None, :] / angles
    shifts = np.arange(-TOP_SHIFT, TOP_SHIFT + 1, dtype=np.float64)[:, None, None]
    tables = []
    for along in (np.cos(theta), np.sin(theta)):
        phase = 2.0 * np.pi * radius * along / IMG * shifts
        tables.append(np.stack([np.cos(phase), np.sin(phase)], axis=1))
    return np.stack(tables).astype(np.float32)


def align_kernel(
    index_hbm,
    rot_hbm,
    shift_hbm,
    stack_hbm,
    table_hbm,
    ctf_hbm,
    class_hbm,
    averages_hbm,
    out_ref,
    rows_ref,
    turned_ref,
    other_ref,
    table_ref,
    index_ref,
    rot_ref,
    shift_ref,
    ctf_ref,
    class_ref,
    averages_ref,
    row_sems,
    sems,
):
    cycles, angles = table_ref.shape[3], table_ref.shape[4]
    grid_rows = 2 * cycles
    count = rows_ref.shape[0]
    chunks = count // BATCH
    owned = averages_ref.shape[0]
    pitch = grid_rows + PAD
    pairs = (
        (index_hbm, index_ref),
        (table_hbm, table_ref),
        (rot_hbm, rot_ref),
        (shift_hbm, shift_ref),
        (ctf_hbm, ctf_ref),
        (class_hbm, class_ref),
        (averages_hbm, averages_ref),
    )
    copies = [pltpu.make_async_copy(a, b, sems.at[n]) for n, (a, b) in enumerate(pairs)]
    for copy in copies:
        copy.start()
    copies[0].wait()

    def issue(i):
        for j in range(BATCH):
            pltpu.make_async_copy(
                stack_hbm.at[index_ref[i * BATCH + j]], rows_ref.at[i * BATCH + j], row_sems.at[i]
            ).start()

    issue(0)
    issue(1)
    for copy in copies[2:]:
        copy.wait()

    classes = (class_ref[...] - HALF_CLASSES).astype(jnp.float32)
    gamma = ctf_ref[...].astype(jnp.float32)
    turned_ref[0:grid_rows, :] = jnp.broadcast_to(classes, (grid_rows, angles))
    turned_ref[pitch : pitch + cycles, :] = gamma
    turned_ref[pitch + cycles : pitch + grid_rows, :] = gamma
    for j in range(owned):
        turned_ref[(2 + j) * pitch : (2 + j) * pitch + grid_rows, :] = averages_ref[j]
    for j in range(2 + owned, AUX):
        turned_ref[j * pitch : j * pitch + grid_rows, :] = jnp.zeros(
            (grid_rows, angles), jnp.float32
        )

    def spread_aux(r, carry):
        got = turned_ref[pl.ds(r, AUX, stride=pitch), :]
        out_ref[r, pl.ds(count, AUX), :] = got.astype(jnp.bfloat16)
        return carry

    lax.fori_loop(0, grid_rows, spread_aux, 0, unroll=32)
    copies[1].wait()

    def turn(i, turned):
        first = i * BATCH
        if i + 2 < chunks:
            issue(i + 2)
        pltpu.make_async_copy(
            stack_hbm.at[pl.ds(0, BATCH)], rows_ref.at[pl.ds(first, BATCH)], row_sems.at[i]
        ).wait()
        for j in range(BATCH):
            particle = first + j
            sx = shift_ref[0, particle] + TOP_SHIFT
            sy = shift_ref[1, particle] + TOP_SHIFT
            back = (angles - 2 * rot_ref[particle]) % angles
            xr, xi = table_ref[0, sx, 0], table_ref[0, sx, 1]
            yr, yi = table_ref[1, sy, 0], table_ref[1, sy, 1]
            cosine = xr * yr - xi * yi
            sine = xr * yi + xi * yr
            real = rows_ref[particle, 0].astype(jnp.float32)
            imag = rows_ref[particle, 1].astype(jnp.float32)
            base = j * pitch
            turned[base : base + cycles, :] = pltpu.roll(cosine * real - sine * imag, back, 1)
            turned[base + cycles : base + grid_rows, :] = pltpu.roll(
                sine * real + cosine * imag, back, 1
            )

    def spread(i, turned):
        first = i * BATCH
        for r in range(grid_rows):
            got = turned[pl.ds(r, BATCH, stride=pitch), :]
            out_ref[r, pl.ds(first, BATCH), :] = got.astype(jnp.bfloat16)

    scratches = (turned_ref, other_ref)
    turn(0, scratches[0])
    for i in range(1, chunks):
        turn(i, scratches[i % 2])
        spread(i - 1, scratches[(i - 1) % 2])
    spread(chunks - 1, scratches[(chunks - 1) % 2])


def align(stack, batch_index, best_class, best_rot, best_shift, ctf, averages):
    count = batch_index.shape[0]
    cycles, angles = stack.shape[2], stack.shape[3]
    grid_rows = 2 * cycles
    owned = averages.shape[0]
    table = jnp.asarray(phase_tables(cycles, angles))
    operands = (
        batch_index,
        best_rot,
        best_shift.T,
        stack,
        table,
        ctf.T,
        best_class.reshape(1, count),
        averages.reshape(owned, grid_rows, angles),
    )
    return pl.pallas_call(
        align_kernel,
        out_shape=jax.ShapeDtypeStruct((grid_rows, count + AUX, angles), jnp.bfloat16),
        in_specs=[pl.BlockSpec(memory_space=pltpu.HBM)] * len(operands),
        out_specs=pl.BlockSpec(memory_space=pltpu.VMEM),
        scratch_shapes=[
            pltpu.VMEM((count, 2, cycles, angles), jnp.bfloat16),
            pltpu.VMEM((BATCH * (grid_rows + PAD), angles), jnp.float32),
            pltpu.VMEM((BATCH * (grid_rows + PAD), angles), jnp.float32),
            pltpu.VMEM(table.shape, jnp.float32),
            pltpu.SMEM((count,), jnp.int32),
            pltpu.SMEM((count,), jnp.int32),
            pltpu.SMEM((2, count), jnp.int32),
            pltpu.VMEM((cycles, count), jnp.bfloat16),
            pltpu.VMEM((1, count), jnp.int32),
            pltpu.VMEM((owned, grid_rows, angles), jnp.float32),
            pltpu.SemaphoreType.DMA((count // BATCH,)),
            pltpu.SemaphoreType.DMA((7,)),
        ],
        compiler_params=pltpu.CompilerParams(vmem_limit_bytes=48 << 20),
        name="align",
    )(*[pltpu.with_memory_space_constraint(x, pltpu.HBM) for x in operands])


def classes_kernel(
    received_ref,
    out_ref,
    aux32_ref,
    class_ref,
    gamma_ref,
    model_ref,
    turned_model_ref,
    sums_ref,
    grads_ref,
    weights_ref,
    error_ref,
    table_ref,
    back_ref,
):
    devices, height, angles = received_ref.shape
    count = height - AUX
    classes = model_ref.shape[0]
    owned = classes // devices
    aux = received_ref[:, count:height, :]
    aux32_ref[...] = aux.astype(jnp.float32).reshape(devices * AUX, angles)
    class_ref[...] = aux32_ref[pl.ds(0, devices, stride=AUX), :]
    gamma_ref[...] = aux32_ref[pl.ds(1, devices, stride=AUX), :]
    for j in range(owned):
        model_ref[pl.ds(j, devices, stride=owned), :] = aux32_ref[
            pl.ds(2 + j, devices, stride=AUX), :
        ]
    turned_model_ref[...] = model_ref[...].T.astype(jnp.bfloat16)
    sums_ref[...] = jnp.zeros(sums_ref.shape, jnp.float32)

    def step(i, carry):
        first = pl.multiple_of(i * SOURCES, SOURCES)
        class_block = class_ref[pl.ds(first, SOURCES), :]
        gamma_block = gamma_ref[pl.ds(first, SOURCES), :]
        down = lax.broadcasted_iota(jnp.int32, (classes, count), 0) - HALF_CLASSES
        down = down.astype(jnp.float32).astype(jnp.bfloat16)
        zero = jnp.zeros((), jnp.bfloat16)
        errors = []
        for pair in range(SOURCES // 2):
            tables = []
            for b in (2 * pair, 2 * pair + 1):
                name = class_block[b : b + 1, :].astype(jnp.bfloat16)
                gamma = gamma_block[b : b + 1, :]
                tables.append(jnp.where(down == name, gamma.astype(jnp.bfloat16), zero))
            table = jnp.concatenate(tables, axis=1)
            rows = received_ref[pl.ds(first + 2 * pair, 2), 0:count, :].reshape(2 * count, angles)
            turned = rows.T.astype(jnp.float32)
            resid = turned - jnp.dot(
                turned_model_ref[...], table, preferred_element_type=jnp.float32
            )
            error = jnp.sum(resid * resid, axis=0, keepdims=True)
            errors += [error[:, 0:count], error[:, count : 2 * count]]
            table_ref[:, 2 * pair * count : 2 * (pair + 1) * count] = table
        columns = [
            jnp.broadcast_to(gamma_block[b : b + 1, :], (SPARE, count)).T for b in range(SOURCES)
        ]
        rows = received_ref[pl.ds(first, SOURCES), 0:count, :].reshape(SOURCES * count, angles)
        columns = jnp.concatenate(columns, axis=0).astype(jnp.bfloat16)
        sums_ref[...] += jnp.dot(
            table_ref[...],
            jnp.concatenate([rows, columns], axis=1),
            preferred_element_type=jnp.float32,
        )
        error_ref[pl.ds(first, SOURCES), :] = jnp.concatenate(errors, axis=0)
        return carry

    lax.fori_loop(0, devices // SOURCES, step, 0, unroll=8)

    weights = jnp.broadcast_to(sums_ref[:, angles : angles + 1], (classes, angles))
    sums = sums_ref[:, 0:angles]
    pull = weights * model_ref[...]
    excess = (pull * (sums + sums - pull)).astype(jnp.bfloat16)
    excess = jnp.dot(
        excess, jnp.ones((angles, angles), jnp.bfloat16), preferred_element_type=jnp.float32
    )
    raw = (excess < 0.0).astype(jnp.float32)
    grads_ref[...] = jnp.where(excess < 0.0, sums, sums - pull)
    share = angles // owned
    part = lax.broadcasted_iota(jnp.int32, (classes, angles), 1) % share // (share // 4)
    high = weights.astype(jnp.bfloat16).astype(jnp.float32)
    weights_ref[...] = jnp.where(part == 0, high, jnp.where(part == 1, weights - high, raw))
    lane = lax.broadcasted_iota(jnp.int32, (devices, angles), 1) // share
    packed = jnp.zeros((devices, angles), jnp.float32)
    back = owned + 2
    for j in range(owned):
        back_ref[pl.ds(j, devices, stride=back), :] = grads_ref[pl.ds(j, devices, stride=owned), :]
        packed = jnp.where(lane == j, weights_ref[pl.ds(j, devices, stride=owned), :], packed)
    back_ref[pl.ds(owned, devices, stride=back), :] = packed
    back_ref[pl.ds(owned + 1, devices, stride=back), :] = error_ref[...]
    out_ref[...] = back_ref[...].astype(jnp.bfloat16)


def class_sums(received, owned):
    devices, height, angles = received.shape
    count = height - AUX
    classes = owned * devices
    return pl.pallas_call(
        classes_kernel,
        out_shape=jax.ShapeDtypeStruct((devices * (owned + 2), angles), jnp.bfloat16),
        in_specs=[pl.BlockSpec(memory_space=pltpu.VMEM)],
        out_specs=pl.BlockSpec(memory_space=pltpu.VMEM),
        scratch_shapes=[
            pltpu.VMEM((devices * AUX, angles), jnp.float32),
            pltpu.VMEM((devices, count), jnp.float32),
            pltpu.VMEM((devices, count), jnp.float32),
            pltpu.VMEM((classes, angles), jnp.float32),
            pltpu.VMEM((angles, classes), jnp.bfloat16),
            pltpu.VMEM((classes, angles + SPARE), jnp.float32),
            pltpu.VMEM((classes, angles), jnp.float32),
            pltpu.VMEM((classes, angles), jnp.float32),
            pltpu.VMEM((devices, count), jnp.float32),
            pltpu.VMEM((classes, SOURCES * count), jnp.bfloat16),
            pltpu.VMEM((devices * (owned + 2), angles), jnp.float32),
        ],
        compiler_params=pltpu.CompilerParams(vmem_limit_bytes=48 << 20),
        name="class_sums",
    )(received)


def update_kernel(
    sent_ref,
    averages_ref,
    velocity_ref,
    new_averages_ref,
    new_velocity_ref,
    error_ref,
    back_ref,
):
    owned, grid_rows, angles = averages_ref.shape
    share = angles // owned
    pitch = owned + 2
    back_ref[...] = sent_ref[...].astype(jnp.float32)
    packed = back_ref[pl.ds(owned, grid_rows, stride=pitch), :]
    for j in range(owned):
        base = j * share
        high = packed[:, base : base + 1]
        low = packed[:, base + share // 4 : base + share // 4 + 1]
        raw = packed[:, base + share // 2 : base + share // 2 + 1]
        weights = jnp.broadcast_to(high + low, (grid_rows, angles))
        old = averages_ref[j]
        model = old.astype(jnp.bfloat16).astype(jnp.float32)
        sent = back_ref[pl.ds(j, grid_rows, stride=pitch), :]
        grads = sent - jnp.broadcast_to(raw * (high + low), (grid_rows, angles)) * model
        step = (grads - RIDGE * old) / (weights + RIDGE)
        moved = MOMENTUM * velocity_ref[j] + step
        new_velocity_ref[j] = moved
        new_averages_ref[j] = old + RATE * moved
    parts = back_ref[pl.ds(owned + 1, grid_rows, stride=pitch), :]
    error_ref[...] = jnp.sum(parts, axis=0, keepdims=True) / (grid_rows * angles)


def update(back, averages, velocity, count):
    owned = averages.shape[0]
    grid_rows, angles = 2 * averages.shape[2], averages.shape[3]
    flat = (owned, grid_rows, angles)
    new_averages, new_velocity, errors = pl.pallas_call(
        update_kernel,
        out_shape=(
            jax.ShapeDtypeStruct(flat, jnp.float32),
            jax.ShapeDtypeStruct(flat, jnp.float32),
            jax.ShapeDtypeStruct((1, count), jnp.float32),
        ),
        scratch_shapes=[pltpu.VMEM(back.shape, jnp.float32)],
        compiler_params=pltpu.CompilerParams(vmem_limit_bytes=48 << 20),
        name="update",
    )(back, averages.reshape(flat), velocity.reshape(flat))
    return (
        new_averages.reshape(averages.shape),
        new_velocity.reshape(averages.shape),
        errors.reshape(count),
    )


def on_device(stack, batch_index, best_class, best_rot, best_shift, ctf, averages, velocity):
    everyone = ("dom", "cls")
    sent = align(stack, batch_index, best_class, best_rot, best_shift, ctf, averages)
    received = lax.all_to_all(sent, everyone, split_axis=0, concat_axis=0, tiled=True)
    partial = class_sums(received, averages.shape[0])
    height, angles = partial.shape
    partial = partial.reshape(height // 2, 2, angles)
    back = lax.all_to_all(partial, everyone, split_axis=0, concat_axis=0, tiled=True)
    back = back.reshape(height, angles)
    return update(back, averages, velocity, batch_index.shape[0])


def solution(mesh):
    whole = ("dom", "cls")
    in_specs = (
        P(whole, None, None, None),
        P(whole),
        P(whole),
        P(whole),
        P(whole, None),
        P(whole, None),
        P(whole, None, None, None),
        P(whole, None, None, None),
    )
    out_specs = (P(whole, None, None, None), P(whole, None, None, None), P(whole))
    return jax.shard_map(
        on_device, mesh=mesh, in_specs=in_specs, out_specs=out_specs, check_vma=False
    )
```

```python
import numpy as np
import jax
import jax.numpy as jnp
from jax import lax
from jax.experimental import pallas as pl
from jax.experimental.pallas import tpu as pltpu
from jax.sharding import PartitionSpec as P

IMG = 128
TOP_SHIFT = 4
MOMENTUM = 0.9
RATE = 0.5
RIDGE = 1.0
BATCH = 16
SOURCES = 16
AUX = 8
PAD = 8
SPARE = 8
HALF_CLASSES = 256


def phase_tables(cycles, angles):
    radius = np.arange(1, cycles + 1, dtype=np.float64)[:, None]
    theta = 2.0 * np.pi * np.arange(angles, dtype=np.float64)[None, :] / angles
    shifts = np.arange(-TOP_SHIFT, TOP_SHIFT + 1, dtype=np.float64)[:, None, None]
    tables = []
    for along in (np.cos(theta), np.sin(theta)):
        phase = 2.0 * np.pi * radius * along / IMG * shifts
        tables.append(np.stack([np.cos(phase), np.sin(phase)], axis=1))
    return np.stack(tables).astype(np.float32)


def align_kernel(
    index_hbm,
    rot_hbm,
    shift_hbm,
    stack_hbm,
    table_hbm,
    ctf_hbm,
    class_hbm,
    averages_hbm,
    out_ref,
    rows_ref,
    turned_ref,
    other_ref,
    table_ref,
    index_ref,
    rot_ref,
    shift_ref,
    ctf_ref,
    class_ref,
    averages_ref,
    row_sems,
    sems,
):
    cycles, angles = table_ref.shape[3], table_ref.shape[4]
    grid_rows = 2 * cycles
    count = rows_ref.shape[0]
    chunks = count // BATCH
    owned = averages_ref.shape[0]
    pitch = BATCH + PAD
    pairs = (
        (index_hbm, index_ref),
        (table_hbm, table_ref),
        (rot_hbm, rot_ref),
        (shift_hbm, shift_ref),
        (ctf_hbm, ctf_ref),
        (class_hbm, class_ref),
        (averages_hbm, averages_ref),
    )
    copies = [pltpu.make_async_copy(a, b, sems.at[n]) for n, (a, b) in enumerate(pairs)]
    for copy in copies:
        copy.start()
    copies[0].wait()

    def issue(i):
        for j in range(BATCH):
            pltpu.make_async_copy(
                stack_hbm.at[index_ref[i * BATCH + j]], rows_ref.at[i * BATCH + j], row_sems.at[i]
            ).start()

    issue(0)
    issue(1)
    for copy in copies[2:]:
        copy.wait()

    classes = (class_ref[...] - HALF_CLASSES).astype(jnp.float32)
    gamma = ctf_ref[...].astype(jnp.float32)
    def place(turned, row, column, values):
        turned[pl.ds(row * pitch + column, values.shape[0], stride=pitch), :] = values

    place(turned_ref, 0, 0, jnp.broadcast_to(classes, (grid_rows, angles)))
    place(turned_ref, 0, 1, gamma)
    place(turned_ref, cycles, 1, gamma)
    for j in range(owned):
        place(turned_ref, 0, 2 + j, averages_ref[j])
    for j in range(2 + owned, AUX):
        place(turned_ref, 0, j, jnp.zeros((grid_rows, angles), jnp.float32))

    for r in range(grid_rows):
        got = turned_ref[r * pitch : r * pitch + AUX, :]
        out_ref[r, count : count + AUX, :] = got.astype(jnp.bfloat16)
    copies[1].wait()

    def turn(i, turned):
        first = i * BATCH
        if i + 2 < chunks:
            issue(i + 2)
        pltpu.make_async_copy(
            stack_hbm.at[pl.ds(0, BATCH)], rows_ref.at[pl.ds(first, BATCH)], row_sems.at[i]
        ).wait()
        for j in range(BATCH):
            particle = first + j
            sx = shift_ref[0, particle] + TOP_SHIFT
            sy = shift_ref[1, particle] + TOP_SHIFT
            back = (angles - 2 * rot_ref[particle]) % angles
            xr, xi = table_ref[0, sx, 0], table_ref[0, sx, 1]
            yr, yi = table_ref[1, sy, 0], table_ref[1, sy, 1]
            cosine = xr * yr - xi * yi
            sine = xr * yi + xi * yr
            real = rows_ref[particle, 0].astype(jnp.float32)
            imag = rows_ref[particle, 1].astype(jnp.float32)
            place(turned, 0, j, pltpu.roll(cosine * real - sine * imag, back, 1))
            place(turned, cycles, j, pltpu.roll(sine * real + cosine * imag, back, 1))

    def spread(i, turned):
        first = i * BATCH
        for r in range(grid_rows):
            got = turned[r * pitch : r * pitch + BATCH, :]
            out_ref[r, pl.ds(first, BATCH), :] = got.astype(jnp.bfloat16)

    scratches = (turned_ref, other_ref)
    turn(0, scratches[0])
    for i in range(1, chunks):
        turn(i, scratches[i % 2])
        spread(i - 1, scratches[(i - 1) % 2])
    spread(chunks - 1, scratches[(chunks - 1) % 2])


def align(stack, batch_index, best_class, best_rot, best_shift, ctf, averages):
    count = batch_index.shape[0]
    cycles, angles = stack.shape[2], stack.shape[3]
    grid_rows = 2 * cycles
    owned = averages.shape[0]
    table = jnp.asarray(phase_tables(cycles, angles))
    operands = (
        batch_index,
        best_rot,
        best_shift.T,
        stack,
        table,
        ctf.T,
        best_class.reshape(1, count),
        averages.reshape(owned, grid_rows, angles),
    )
    return pl.pallas_call(
        align_kernel,
        out_shape=jax.ShapeDtypeStruct((grid_rows, count + AUX, angles), jnp.bfloat16),
        in_specs=[pl.BlockSpec(memory_space=pltpu.HBM)] * len(operands),
        out_specs=pl.BlockSpec(memory_space=pltpu.VMEM),
        scratch_shapes=[
            pltpu.VMEM((count, 2, cycles, angles), jnp.bfloat16),
            pltpu.VMEM((grid_rows * (BATCH + PAD), angles), jnp.float32),
            pltpu.VMEM((grid_rows * (BATCH + PAD), angles), jnp.float32),
            pltpu.VMEM(table.shape, jnp.float32),
            pltpu.SMEM((count,), jnp.int32),
            pltpu.SMEM((count,), jnp.int32),
            pltpu.SMEM((2, count), jnp.int32),
            pltpu.VMEM((cycles, count), jnp.bfloat16),
            pltpu.VMEM((1, count), jnp.int32),
            pltpu.VMEM((owned, grid_rows, angles), jnp.float32),
            pltpu.SemaphoreType.DMA((count // BATCH,)),
            pltpu.SemaphoreType.DMA((7,)),
        ],
        compiler_params=pltpu.CompilerParams(vmem_limit_bytes=48 << 20),
        name="align",
    )(*[pltpu.with_memory_space_constraint(x, pltpu.HBM) for x in operands])


def classes_kernel(
    received_ref,
    out_ref,
    aux32_ref,
    class_ref,
    gamma_ref,
    model_ref,
    turned_model_ref,
    sums_ref,
    grads_ref,
    weights_ref,
    error_ref,
    table_ref,
    back_ref,
):
    devices, height, angles = received_ref.shape
    count = height - AUX
    classes = model_ref.shape[0]
    owned = classes // devices
    aux = received_ref[:, count:height, :]
    aux32_ref[...] = aux.astype(jnp.float32).reshape(devices * AUX, angles)
    class_ref[...] = aux32_ref[pl.ds(0, devices, stride=AUX), :]
    gamma_ref[...] = aux32_ref[pl.ds(1, devices, stride=AUX), :]
    for j in range(owned):
        model_ref[pl.ds(j, devices, stride=owned), :] = aux32_ref[
            pl.ds(2 + j, devices, stride=AUX), :
        ]
    turned_model_ref[...] = model_ref[...].T.astype(jnp.bfloat16)
    sums_ref[...] = jnp.zeros(sums_ref.shape, jnp.float32)

    def step(i, carry):
        first = pl.multiple_of(i * SOURCES, SOURCES)
        class_block = class_ref[pl.ds(first, SOURCES), :]
        gamma_block = gamma_ref[pl.ds(first, SOURCES), :]
        down = lax.broadcasted_iota(jnp.int32, (classes, count), 0) - HALF_CLASSES
        down = down.astype(jnp.float32).astype(jnp.bfloat16)
        zero = jnp.zeros((), jnp.bfloat16)
        errors = []
        for pair in range(SOURCES // 2):
            tables = []
            for b in (2 * pair, 2 * pair + 1):
                name = class_block[b : b + 1, :].astype(jnp.bfloat16)
                gamma = gamma_block[b : b + 1, :]
                tables.append(jnp.where(down == name, gamma.astype(jnp.bfloat16), zero))
            table = jnp.concatenate(tables, axis=1)
            rows = received_ref[pl.ds(first + 2 * pair, 2), 0:count, :].reshape(2 * count, angles)
            turned = rows.T.astype(jnp.float32)
            resid = turned - jnp.dot(
                turned_model_ref[...], table, preferred_element_type=jnp.float32
            )
            error = jnp.sum(resid * resid, axis=0, keepdims=True)
            errors += [error[:, 0:count], error[:, count : 2 * count]]
            table_ref[:, 2 * pair * count : 2 * (pair + 1) * count] = table
        columns = [
            jnp.broadcast_to(gamma_block[b : b + 1, :], (SPARE, count)).T for b in range(SOURCES)
        ]
        rows = received_ref[pl.ds(first, SOURCES), 0:count, :].reshape(SOURCES * count, angles)
        columns = jnp.concatenate(columns, axis=0).astype(jnp.bfloat16)
        sums_ref[...] += jnp.dot(
            table_ref[...],
            jnp.concatenate([rows, columns], axis=1),
            preferred_element_type=jnp.float32,
        )
        error_ref[pl.ds(first, SOURCES), :] = jnp.concatenate(errors, axis=0)
        return carry

    lax.fori_loop(0, devices // SOURCES, step, 0, unroll=8)

    weights = jnp.broadcast_to(sums_ref[:, angles : angles + 1], (classes, angles))
    sums = sums_ref[:, 0:angles]
    pull = weights * model_ref[...]
    excess = (pull * (sums + sums - pull)).astype(jnp.bfloat16)
    excess = jnp.dot(
        excess, jnp.ones((angles, angles), jnp.bfloat16), preferred_element_type=jnp.float32
    )
    raw = (excess < 0.0).astype(jnp.float32)
    grads_ref[...] = jnp.where(excess < 0.0, sums, sums - pull)
    share = angles // owned
    part = lax.broadcasted_iota(jnp.int32, (classes, angles), 1) % share // (share // 4)
    high = weights.astype(jnp.bfloat16).astype(jnp.float32)
    weights_ref[...] = jnp.where(part == 0, high, jnp.where(part == 1, weights - high, raw))
    lane = lax.broadcasted_iota(jnp.int32, (devices, angles), 1) // share
    packed = jnp.zeros((devices, angles), jnp.float32)
    back = owned + 2
    for j in range(owned):
        back_ref[pl.ds(j, devices, stride=back), :] = grads_ref[pl.ds(j, devices, stride=owned), :]
        packed = jnp.where(lane == j, weights_ref[pl.ds(j, devices, stride=owned), :], packed)
    back_ref[pl.ds(owned, devices, stride=back), :] = packed
    back_ref[pl.ds(owned + 1, devices, stride=back), :] = error_ref[...]
    out_ref[...] = back_ref[...].astype(jnp.bfloat16)


def class_sums(received, owned):
    devices, height, angles = received.shape
    count = height - AUX
    classes = owned * devices
    return pl.pallas_call(
        classes_kernel,
        out_shape=jax.ShapeDtypeStruct((devices * (owned + 2), angles), jnp.bfloat16),
        in_specs=[pl.BlockSpec(memory_space=pltpu.VMEM)],
        out_specs=pl.BlockSpec(memory_space=pltpu.VMEM),
        scratch_shapes=[
            pltpu.VMEM((devices * AUX, angles), jnp.float32),
            pltpu.VMEM((devices, count), jnp.float32),
            pltpu.VMEM((devices, count), jnp.float32),
            pltpu.VMEM((classes, angles), jnp.float32),
            pltpu.VMEM((angles, classes), jnp.bfloat16),
            pltpu.VMEM((classes, angles + SPARE), jnp.float32),
            pltpu.VMEM((classes, angles), jnp.float32),
            pltpu.VMEM((classes, angles), jnp.float32),
            pltpu.VMEM((devices, count), jnp.float32),
            pltpu.VMEM((classes, SOURCES * count), jnp.bfloat16),
            pltpu.VMEM((devices * (owned + 2), angles), jnp.float32),
        ],
        compiler_params=pltpu.CompilerParams(vmem_limit_bytes=48 << 20),
        name="class_sums",
    )(received)


def update_kernel(
    sent_ref,
    averages_ref,
    velocity_ref,
    new_averages_ref,
    new_velocity_ref,
    error_ref,
    back_ref,
):
    owned, grid_rows, angles = averages_ref.shape
    share = angles // owned
    pitch = owned + 2
    back_ref[...] = sent_ref[...].astype(jnp.float32)
    packed = back_ref[pl.ds(owned, grid_rows, stride=pitch), :]
    for j in range(owned):
        base = j * share
        high = packed[:, base : base + 1]
        low = packed[:, base + share // 4 : base + share // 4 + 1]
        raw = packed[:, base + share // 2 : base + share // 2 + 1]
        weights = jnp.broadcast_to(high + low, (grid_rows, angles))
        old = averages_ref[j]
        model = old.astype(jnp.bfloat16).astype(jnp.float32)
        sent = back_ref[pl.ds(j, grid_rows, stride=pitch), :]
        grads = sent - jnp.broadcast_to(raw * (high + low), (grid_rows, angles)) * model
        step = (grads - RIDGE * old) / (weights + RIDGE)
        moved = MOMENTUM * velocity_ref[j] + step
        new_velocity_ref[j] = moved
        new_averages_ref[j] = old + RATE * moved
    parts = back_ref[pl.ds(owned + 1, grid_rows, stride=pitch), :]
    error_ref[...] = jnp.sum(parts, axis=0, keepdims=True) / (grid_rows * angles)


def update(back, averages, velocity, count):
    owned = averages.shape[0]
    grid_rows, angles = 2 * averages.shape[2], averages.shape[3]
    flat = (owned, grid_rows, angles)
    new_averages, new_velocity, errors = pl.pallas_call(
        update_kernel,
        out_shape=(
            jax.ShapeDtypeStruct(flat, jnp.float32),
            jax.ShapeDtypeStruct(flat, jnp.float32),
            jax.ShapeDtypeStruct((1, count), jnp.float32),
        ),
        scratch_shapes=[pltpu.VMEM(back.shape, jnp.float32)],
        compiler_params=pltpu.CompilerParams(vmem_limit_bytes=48 << 20),
        name="update",
    )(back, averages.reshape(flat), velocity.reshape(flat))
    return (
        new_averages.reshape(averages.shape),
        new_velocity.reshape(averages.shape),
        errors.reshape(count),
    )


def on_device(stack, batch_index, best_class, best_rot, best_shift, ctf, averages, velocity):
    everyone = ("dom", "cls")
    sent = align(stack, batch_index, best_class, best_rot, best_shift, ctf, averages)
    received = lax.all_to_all(sent, everyone, split_axis=0, concat_axis=0, tiled=True)
    partial = class_sums(received, averages.shape[0])
    height, angles = partial.shape
    partial = partial.reshape(height // 2, 2, angles)
    back = lax.all_to_all(partial, everyone, split_axis=0, concat_axis=0, tiled=True)
    back = back.reshape(height, angles)
    return update(back, averages, velocity, batch_index.shape[0])


def solution(mesh):
    whole = ("dom", "cls")
    in_specs = (
        P(whole, None, None, None),
        P(whole),
        P(whole),
        P(whole),
        P(whole, None),
        P(whole, None),
        P(whole, None, None, None),
        P(whole, None, None, None),
    )
    out_specs = (P(whole, None, None, None), P(whole, None, None, None), P(whole))
    return jax.shard_map(
        on_device, mesh=mesh, in_specs=in_specs, out_specs=out_specs, check_vma=False
    )
```

```python
import numpy as np
import jax
import jax.numpy as jnp
from jax import lax
from jax.experimental import pallas as pl
from jax.experimental.pallas import tpu as pltpu
from jax.sharding import PartitionSpec as P

IMG = 128
TOP_SHIFT = 4
MOMENTUM = 0.9
RATE = 0.5
RIDGE = 1.0
BATCH = 32
SOURCES = 16
AUX = 8
PAD = 8
SPARE = 8
HALF_CLASSES = 256


def phase_tables(cycles, angles):
    radius = np.arange(1, cycles + 1, dtype=np.float64)[:, None]
    theta = 2.0 * np.pi * np.arange(angles, dtype=np.float64)[None, :] / angles
    shifts = np.arange(-TOP_SHIFT, TOP_SHIFT + 1, dtype=np.float64)[:, None, None]
    tables = []
    for along in (np.cos(theta), np.sin(theta)):
        phase = 2.0 * np.pi * radius * along / IMG * shifts
        tables.append(np.stack([np.cos(phase), np.sin(phase)], axis=1))
    return np.stack(tables).astype(np.float32)


def align_kernel(
    index_hbm,
    rot_hbm,
    shift_hbm,
    stack_hbm,
    table_hbm,
    ctf_hbm,
    class_hbm,
    averages_hbm,
    out_ref,
    rows_ref,
    turned_ref,
    other_ref,
    table_ref,
    index_ref,
    rot_ref,
    shift_ref,
    ctf_ref,
    class_ref,
    averages_ref,
    row_sems,
    sems,
):
    cycles, angles = table_ref.shape[3], table_ref.shape[4]
    grid_rows = 2 * cycles
    count = rows_ref.shape[0]
    chunks = count // BATCH
    owned = averages_ref.shape[0]
    pitch = BATCH + PAD
    pairs = (
        (index_hbm, index_ref),
        (table_hbm, table_ref),
        (rot_hbm, rot_ref),
        (shift_hbm, shift_ref),
        (ctf_hbm, ctf_ref),
        (class_hbm, class_ref),
        (averages_hbm, averages_ref),
    )
    copies = [pltpu.make_async_copy(a, b, sems.at[n]) for n, (a, b) in enumerate(pairs)]
    for copy in copies:
        copy.start()
    copies[0].wait()

    def issue(i):
        for j in range(BATCH):
            pltpu.make_async_copy(
                stack_hbm.at[index_ref[i * BATCH + j]], rows_ref.at[i * BATCH + j], row_sems.at[i]
            ).start()

    issue(0)
    issue(1)
    for copy in copies[2:]:
        copy.wait()

    classes = (class_ref[...] - HALF_CLASSES).astype(jnp.float32)
    gamma = ctf_ref[...].astype(jnp.float32)
    def place(turned, row, column, values):
        turned[pl.ds(row * pitch + column, values.shape[0], stride=pitch), :] = values

    place(turned_ref, 0, 0, jnp.broadcast_to(classes, (grid_rows, angles)))
    place(turned_ref, 0, 1, gamma)
    place(turned_ref, cycles, 1, gamma)
    for j in range(owned):
        place(turned_ref, 0, 2 + j, averages_ref[j])
    for j in range(2 + owned, AUX):
        place(turned_ref, 0, j, jnp.zeros((grid_rows, angles), jnp.float32))

    for r in range(grid_rows):
        got = turned_ref[r * pitch : r * pitch + AUX, :]
        out_ref[r, count : count + AUX, :] = got.astype(jnp.bfloat16)
    copies[1].wait()

    def turn(i, turned):
        first = i * BATCH
        if i + 2 < chunks:
            issue(i + 2)
        pltpu.make_async_copy(
            stack_hbm.at[pl.ds(0, BATCH)], rows_ref.at[pl.ds(first, BATCH)], row_sems.at[i]
        ).wait()
        for j in range(BATCH):
            particle = first + j
            sx = shift_ref[0, particle] + TOP_SHIFT
            sy = shift_ref[1, particle] + TOP_SHIFT
            back = (angles - 2 * rot_ref[particle]) % angles
            xr, xi = table_ref[0, sx, 0], table_ref[0, sx, 1]
            yr, yi = table_ref[1, sy, 0], table_ref[1, sy, 1]
            cosine = xr * yr - xi * yi
            sine = xr * yi + xi * yr
            real = rows_ref[particle, 0].astype(jnp.float32)
            imag = rows_ref[particle, 1].astype(jnp.float32)
            place(turned, 0, j, pltpu.roll(cosine * real - sine * imag, back, 1))
            place(turned, cycles, j, pltpu.roll(sine * real + cosine * imag, back, 1))

    def spread(i, turned):
        first = i * BATCH
        for r in range(grid_rows):
            got = turned[r * pitch : r * pitch + BATCH, :]
            out_ref[r, pl.ds(first, BATCH), :] = got.astype(jnp.bfloat16)

    scratches = (turned_ref, other_ref)
    turn(0, scratches[0])
    for i in range(1, chunks):
        turn(i, scratches[i % 2])
        spread(i - 1, scratches[(i - 1) % 2])
    spread(chunks - 1, scratches[(chunks - 1) % 2])


def align(stack, batch_index, best_class, best_rot, best_shift, ctf, averages):
    count = batch_index.shape[0]
    cycles, angles = stack.shape[2], stack.shape[3]
    grid_rows = 2 * cycles
    owned = averages.shape[0]
    table = jnp.asarray(phase_tables(cycles, angles))
    operands = (
        batch_index,
        best_rot,
        best_shift.T,
        stack,
        table,
        ctf.T,
        best_class.reshape(1, count),
        averages.reshape(owned, grid_rows, angles),
    )
    return pl.pallas_call(
        align_kernel,
        out_shape=jax.ShapeDtypeStruct((grid_rows, count + AUX, angles), jnp.bfloat16),
        in_specs=[pl.BlockSpec(memory_space=pltpu.HBM)] * len(operands),
        out_specs=pl.BlockSpec(memory_space=pltpu.VMEM),
        scratch_shapes=[
            pltpu.VMEM((count, 2, cycles, angles), jnp.bfloat16),
            pltpu.VMEM((grid_rows * (BATCH + PAD), angles), jnp.float32),
            pltpu.VMEM((grid_rows * (BATCH + PAD), angles), jnp.float32),
            pltpu.VMEM(table.shape, jnp.float32),
            pltpu.SMEM((count,), jnp.int32),
            pltpu.SMEM((count,), jnp.int32),
            pltpu.SMEM((2, count), jnp.int32),
            pltpu.VMEM((cycles, count), jnp.bfloat16),
            pltpu.VMEM((1, count), jnp.int32),
            pltpu.VMEM((owned, grid_rows, angles), jnp.float32),
            pltpu.SemaphoreType.DMA((count // BATCH,)),
            pltpu.SemaphoreType.DMA((7,)),
        ],
        compiler_params=pltpu.CompilerParams(vmem_limit_bytes=48 << 20),
        name="align",
    )(*[pltpu.with_memory_space_constraint(x, pltpu.HBM) for x in operands])


def classes_kernel(
    received_ref,
    out_ref,
    aux32_ref,
    class_ref,
    gamma_ref,
    model_ref,
    turned_model_ref,
    sums_ref,
    grads_ref,
    weights_ref,
    error_ref,
    table_ref,
    back_ref,
):
    devices, height, angles = received_ref.shape
    count = height - AUX
    classes = model_ref.shape[0]
    owned = classes // devices
    aux = received_ref[:, count:height, :]
    aux32_ref[...] = aux.astype(jnp.float32).reshape(devices * AUX, angles)
    class_ref[...] = aux32_ref[pl.ds(0, devices, stride=AUX), :]
    gamma_ref[...] = aux32_ref[pl.ds(1, devices, stride=AUX), :]
    for j in range(owned):
        model_ref[pl.ds(j, devices, stride=owned), :] = aux32_ref[
            pl.ds(2 + j, devices, stride=AUX), :
        ]
    turned_model_ref[...] = model_ref[...].T.astype(jnp.bfloat16)
    sums_ref[...] = jnp.zeros(sums_ref.shape, jnp.float32)

    def step(i, carry):
        first = pl.multiple_of(i * SOURCES, SOURCES)
        class_block = class_ref[pl.ds(first, SOURCES), :]
        gamma_block = gamma_ref[pl.ds(first, SOURCES), :]
        down = lax.broadcasted_iota(jnp.int32, (classes, count), 0) - HALF_CLASSES
        down = down.astype(jnp.float32).astype(jnp.bfloat16)
        zero = jnp.zeros((), jnp.bfloat16)
        errors = []
        for pair in range(SOURCES // 2):
            tables = []
            for b in (2 * pair, 2 * pair + 1):
                name = class_block[b : b + 1, :].astype(jnp.bfloat16)
                gamma = gamma_block[b : b + 1, :]
                tables.append(jnp.where(down == name, gamma.astype(jnp.bfloat16), zero))
            table = jnp.concatenate(tables, axis=1)
            rows = received_ref[pl.ds(first + 2 * pair, 2), 0:count, :].reshape(2 * count, angles)
            turned = rows.T.astype(jnp.float32)
            resid = turned - jnp.dot(
                turned_model_ref[...], table, preferred_element_type=jnp.float32
            )
            error = jnp.sum(resid * resid, axis=0, keepdims=True)
            errors += [error[:, 0:count], error[:, count : 2 * count]]
            table_ref[:, 2 * pair * count : 2 * (pair + 1) * count] = table
        columns = [
            jnp.broadcast_to(gamma_block[b : b + 1, :], (SPARE, count)).T for b in range(SOURCES)
        ]
        rows = received_ref[pl.ds(first, SOURCES), 0:count, :].reshape(SOURCES * count, angles)
        columns = jnp.concatenate(columns, axis=0).astype(jnp.bfloat16)
        sums_ref[...] += jnp.dot(
            table_ref[...],
            jnp.concatenate([rows, columns], axis=1),
            preferred_element_type=jnp.float32,
        )
        error_ref[pl.ds(first, SOURCES), :] = jnp.concatenate(errors, axis=0)
        return carry

    lax.fori_loop(0, devices // SOURCES, step, 0, unroll=8)

    weights = jnp.broadcast_to(sums_ref[:, angles : angles + 1], (classes, angles))
    sums = sums_ref[:, 0:angles]
    pull = weights * model_ref[...]
    excess = (pull * (sums + sums - pull)).astype(jnp.bfloat16)
    excess = jnp.dot(
        excess, jnp.ones((angles, angles), jnp.bfloat16), preferred_element_type=jnp.float32
    )
    raw = (excess < 0.0).astype(jnp.float32)
    grads_ref[...] = jnp.where(excess < 0.0, sums, sums - pull)
    share = angles // owned
    part = lax.broadcasted_iota(jnp.int32, (classes, angles), 1) % share // (share // 4)
    high = weights.astype(jnp.bfloat16).astype(jnp.float32)
    weights_ref[...] = jnp.where(part == 0, high, jnp.where(part == 1, weights - high, raw))
    lane = lax.broadcasted_iota(jnp.int32, (devices, angles), 1) // share
    packed = jnp.zeros((devices, angles), jnp.float32)
    back = owned + 2
    for j in range(owned):
        back_ref[pl.ds(j, devices, stride=back), :] = grads_ref[pl.ds(j, devices, stride=owned), :]
        packed = jnp.where(lane == j, weights_ref[pl.ds(j, devices, stride=owned), :], packed)
    back_ref[pl.ds(owned, devices, stride=back), :] = packed
    back_ref[pl.ds(owned + 1, devices, stride=back), :] = error_ref[...]
    out_ref[...] = back_ref[...].astype(jnp.bfloat16)


def class_sums(received, owned):
    devices, height, angles = received.shape
    count = height - AUX
    classes = owned * devices
    return pl.pallas_call(
        classes_kernel,
        out_shape=jax.ShapeDtypeStruct((devices * (owned + 2), angles), jnp.bfloat16),
        in_specs=[pl.BlockSpec(memory_space=pltpu.VMEM)],
        out_specs=pl.BlockSpec(memory_space=pltpu.VMEM),
        scratch_shapes=[
            pltpu.VMEM((devices * AUX, angles), jnp.float32),
            pltpu.VMEM((devices, count), jnp.float32),
            pltpu.VMEM((devices, count), jnp.float32),
            pltpu.VMEM((classes, angles), jnp.float32),
            pltpu.VMEM((angles, classes), jnp.bfloat16),
            pltpu.VMEM((classes, angles + SPARE), jnp.float32),
            pltpu.VMEM((classes, angles), jnp.float32),
            pltpu.VMEM((classes, angles), jnp.float32),
            pltpu.VMEM((devices, count), jnp.float32),
            pltpu.VMEM((classes, SOURCES * count), jnp.bfloat16),
            pltpu.VMEM((devices * (owned + 2), angles), jnp.float32),
        ],
        compiler_params=pltpu.CompilerParams(vmem_limit_bytes=48 << 20),
        name="class_sums",
    )(received)


def update_kernel(
    sent_ref,
    averages_ref,
    velocity_ref,
    new_averages_ref,
    new_velocity_ref,
    error_ref,
    back_ref,
):
    owned, grid_rows, angles = averages_ref.shape
    share = angles // owned
    pitch = owned + 2
    back_ref[...] = sent_ref[...].astype(jnp.float32)
    packed = back_ref[pl.ds(owned, grid_rows, stride=pitch), :]
    for j in range(owned):
        base = j * share
        high = packed[:, base : base + 1]
        low = packed[:, base + share // 4 : base + share // 4 + 1]
        raw = packed[:, base + share // 2 : base + share // 2 + 1]
        weights = jnp.broadcast_to(high + low, (grid_rows, angles))
        old = averages_ref[j]
        model = old.astype(jnp.bfloat16).astype(jnp.float32)
        sent = back_ref[pl.ds(j, grid_rows, stride=pitch), :]
        grads = sent - jnp.broadcast_to(raw * (high + low), (grid_rows, angles)) * model
        step = (grads - RIDGE * old) / (weights + RIDGE)
        moved = MOMENTUM * velocity_ref[j] + step
        new_velocity_ref[j] = moved
        new_averages_ref[j] = old + RATE * moved
    parts = back_ref[pl.ds(owned + 1, grid_rows, stride=pitch), :]
    error_ref[...] = jnp.sum(parts, axis=0, keepdims=True) / (grid_rows * angles)


def update(back, averages, velocity, count):
    owned = averages.shape[0]
    grid_rows, angles = 2 * averages.shape[2], averages.shape[3]
    flat = (owned, grid_rows, angles)
    new_averages, new_velocity, errors = pl.pallas_call(
        update_kernel,
        out_shape=(
            jax.ShapeDtypeStruct(flat, jnp.float32),
            jax.ShapeDtypeStruct(flat, jnp.float32),
            jax.ShapeDtypeStruct((1, count), jnp.float32),
        ),
        scratch_shapes=[pltpu.VMEM(back.shape, jnp.float32)],
        compiler_params=pltpu.CompilerParams(vmem_limit_bytes=48 << 20),
        name="update",
    )(back, averages.reshape(flat), velocity.reshape(flat))
    return (
        new_averages.reshape(averages.shape),
        new_velocity.reshape(averages.shape),
        errors.reshape(count),
    )


def on_device(stack, batch_index, best_class, best_rot, best_shift, ctf, averages, velocity):
    everyone = ("dom", "cls")
    sent = align(stack, batch_index, best_class, best_rot, best_shift, ctf, averages)
    received = lax.all_to_all(sent, everyone, split_axis=0, concat_axis=0, tiled=True)
    partial = class_sums(received, averages.shape[0])
    height, angles = partial.shape
    partial = partial.reshape(height // 2, 2, angles)
    back = lax.all_to_all(partial, everyone, split_axis=0, concat_axis=0, tiled=True)
    back = back.reshape(height, angles)
    return update(back, averages, velocity, batch_index.shape[0])


def solution(mesh):
    whole = ("dom", "cls")
    in_specs = (
        P(whole, None, None, None),
        P(whole),
        P(whole),
        P(whole),
        P(whole, None),
        P(whole, None),
        P(whole, None, None, None),
        P(whole, None, None, None),
    )
    out_specs = (P(whole, None, None, None), P(whole, None, None, None), P(whole))
    return jax.shard_map(
        on_device, mesh=mesh, in_specs=in_specs, out_specs=out_specs, check_vma=False
    )
```
